1024 devices in a mesh: ctx: 64 (over z_lo, y, core), tp: 4 (over z_hi), rep: 4 (over x).
Axes of the slice: x: 4, y: 4, z: 32 (z_hi: 4, z_lo: 8; z = z_hi * 8 + z_lo), core: 2. Of those that a mesh axis runs over, the one named last changes fastest.
Arguments:
- queries: bfloat16 [49152, 4096], P(('ctx', 'rep'), 'tp'), may hold values from -6 to 6
- key_states: bfloat16 [49152, 1024], P(('ctx', 'rep'), 'tp'), may hold values from -6 to 6
- value_states: bfloat16 [49152, 1024], P(('ctx', 'rep'), 'tp'), may hold values from -6 to 6
- out_grad: bfloat16 [49152, 4096], P(('ctx', 'rep'), 'tp'), may hold values from -6 to 6
- doc_lengths: int32 [255], replicated, may hold values from 0 to 768, as said below
Outputs:
- attended: bfloat16 [49152, 4096], P(('ctx', 'rep'), 'tp')
- query_grad: bfloat16 [49152, 4096], P(('ctx', 'rep'), 'tp')
- key_grad: bfloat16 [49152, 1024], P(('ctx', 'rep'), 'tp')
- value_grad: bfloat16 [49152, 1024], P(('ctx', 'rep'), 'tp')
The draws below stay inside these ranges and needn't reach their ends.
Inputs may be any that keep to these rules, and one draw needn't show every extreme that they name: `doc_lengths`: the lengths sum to 49152; the largest is exactly 768; some entries are 0.
All inputs are finite; a program needn't handle non-finite values.
Results may differ from the reference program's by a relative error of at most 0.007.
Values may be sent and summed in bfloat16 or wider, within the bound.
No kernel may reach another device: no remote copies, remote signals or barrier semaphores. Data moves between devices by JAX's collectives and lax.ppermute only.
A program may use at most 64 MiB of HBM per device.

```python
import math
import jax
import jax.numpy as jnp
from jax import lax

HQ = 32
HK = 8
HD = 128
TOK_DEV = 192
REACH = 4
TOKENS = 49152
MOST = 768


def layout(key):
    folded = jax.random.fold_in(key, 11)
    key_offset, key_cuts, key_whole, key_forced = jax.random.split(folded, 4)
    group_count = TOKENS // MOST - 1
    offset = jax.random.randint(key_offset, (), 1, TOK_DEV)
    cut_points = jnp.sort(jax.random.randint(key_cuts, (group_count, 3), 0, MOST - 1), axis=1)
    whole_flag = jax.random.randint(key_whole, (group_count, 1), 0, 2)
    forced = jax.random.randint(key_forced, (), 0, group_count)
    forced_flag = (jnp.arange(group_count) == forced).astype(jnp.int32)[:, None]
    whole_flag = jnp.maximum(whole_flag, forced_flag)
    cut_points = cut_points * (1 - whole_flag)
    return (offset, cut_points)


def draw_doc_lengths(key, part):
    offset, cut_points = layout(key)
    group_count = cut_points.shape[0]
    edges = jnp.concatenate([jnp.zeros((group_count, 1), jnp.int32), cut_points.astype(jnp.int32), jnp.full((group_count, 1), MOST, jnp.int32)], axis=1)
    pieces = (edges[:, 1:] - edges[:, :-1]).reshape(-1)
    rest_len = TOKENS - offset - group_count * MOST
    first_half = rest_len // 2
    tail_pair = jnp.stack([first_half, rest_len - first_half]).astype(jnp.int32)
    return jnp.concatenate([offset.astype(jnp.int32)[None], pieces, tail_pair]).astype(jnp.int32)


def draw_queries(key, part):
    drawn = jnp.clip(jax.random.normal(jax.random.fold_in(key, 21), (TOKENS, HQ * HD), jnp.float32), -4.0, 4.0)
    return drawn.astype(jnp.bfloat16)


def draw_key_states(key, part):
    drawn = jnp.clip(jax.random.normal(jax.random.fold_in(key, 22), (TOKENS, HK * HD), jnp.float32), -4.0, 4.0)
    return drawn.astype(jnp.bfloat16)


def block_scale(rng, dims, cuts, least, largest):
    factor_of = 1.0
    for dim, parts in cuts:
        steps = jax.random.uniform(jax.random.fold_in(jax.random.fold_in(rng, 6), dim), (parts,), jnp.float32, least / len(cuts), largest / len(cuts))
        factor_of = factor_of * jnp.repeat(jnp.exp(steps), dims[dim] // parts).reshape((-1,) + (1,) * (len(dims) - 1 - dim))
    return factor_of


def centred(stream_key, dims, width, bound, cuts=(), kind=jnp.bfloat16):
    values = jax.random.normal(stream_key, dims, jnp.float32) * width
    if len(cuts) > 0:
        values = block_scale(stream_key, dims, cuts, -0.22, 0.18) * values
    return jnp.clip(values, min=-bound, max=bound).astype(kind)


def setup_inputs(seed: int = 0) -> dict:
    keys = jax.random.split(jax.random.key(seed), 6)
    queries = draw_queries(jax.random.fold_in(keys[5], 71), 0)
    key_states = draw_key_states(jax.random.fold_in(keys[5], 71), 0)
    value_states = centred(keys[2], (TOKENS, HK * HD), 1.0, 6.0, ((0, 256), (1, 4)))
    out_grad = centred(keys[3], (TOKENS, HQ * HD), 1.0, 6.0, ((0, 256), (1, 4)))
    doc_lengths = draw_doc_lengths(jax.random.fold_in(keys[5], 71), 0)
    return dict(queries=queries, key_states=key_states, value_states=value_states, out_grad=out_grad, doc_lengths=doc_lengths)


masked_score = -1e+30

def document_of(doc_ends, positions):
    return lax.optimization_barrier(jnp.sum((doc_ends[None, :] <= positions[:, None]).astype(jnp.int32), axis=1))

def reference(queries, key_states, value_states, out_grad, doc_lengths):
    doc_ends = jnp.cumsum(doc_lengths).astype(jnp.int32)
    kv_heads = key_states.shape[1] // HD
    query_width = queries.shape[1]
    group_size = query_width // HD // kv_heads
    key_width = key_states.shape[1]
    scaling = 1.0 / math.sqrt(HD)
    block_count = TOKENS // TOK_DEV
    window = (REACH + 1) * TOK_DEV
    padding = jnp.zeros((REACH * TOK_DEV, key_width), key_states.dtype)
    key_padded = jnp.concatenate([padding, key_states], axis=0)
    value_padded = jnp.concatenate([padding, value_states], axis=0)
    query_tail = jnp.zeros((REACH * TOK_DEV, query_width), queries.dtype)
    query_padded = jnp.concatenate([queries, query_tail], axis=0)
    grad_padded = jnp.concatenate([out_grad, query_tail.astype(out_grad.dtype)], axis=0)
    highest = lax.Precision.HIGHEST

    def forward_block(block_index):
        start = (block_index * TOK_DEV).astype(jnp.int32)
        query_block = lax.dynamic_slice_in_dim(queries, start, TOK_DEV, 0).astype(jnp.float32)
        query_block = query_block.reshape(TOK_DEV, kv_heads, group_size, HD)
        grad_block = lax.dynamic_slice_in_dim(out_grad, start, TOK_DEV, 0).astype(jnp.float32)
        grad_block = grad_block.reshape(TOK_DEV, kv_heads, group_size, HD)
        key_window = lax.dynamic_slice_in_dim(key_padded, start, window, 0).astype(jnp.float32)
        key_window = key_window.reshape(window, kv_heads, HD)
        value_window = lax.dynamic_slice_in_dim(value_padded, start, window, 0).astype(jnp.float32)
        value_window = value_window.reshape(window, kv_heads, HD)
        query_pos = start + jnp.arange(TOK_DEV, dtype=jnp.int32)
        key_pos = start - REACH * TOK_DEV + jnp.arange(window, dtype=jnp.int32)
        allowed = document_of(doc_ends, key_pos)[None, :] == document_of(doc_ends, query_pos)[:, None]
        allowed = allowed & (key_pos[None, :] <= query_pos[:, None]) & (key_pos[None, :] >= 0)
        scores = jnp.einsum('tgjd,sgd->gjts', query_block, key_window, precision=highest) * scaling
        scores = jnp.where(allowed[None, None], scores, masked_score)
        row_max = lax.optimization_barrier(jnp.max(scores, axis=-1, keepdims=True))
        log_total = row_max + jnp.log(lax.optimization_barrier(jnp.sum(jnp.exp(scores - row_max), axis=-1, keepdims=True)))
        probs = jnp.exp(scores - log_total)
        probs_bf = lax.optimization_barrier(probs.astype(jnp.bfloat16)).astype(jnp.float32)
        attended = jnp.einsum('gjts,sgd->tgjd', probs_bf, value_window, precision=highest)
        attended_bf = lax.optimization_barrier(attended.astype(jnp.bfloat16))
        delta_row = lax.optimization_barrier(jnp.sum(grad_block * attended_bf.astype(jnp.float32), axis=-1))
        dprobs = jnp.einsum('tgjd,sgd->gjts', grad_block, value_window, precision=highest)
        dscores = probs * (dprobs - jnp.transpose(delta_row, (1, 2, 0))[..., None])
        dscores = lax.optimization_barrier(dscores.astype(jnp.bfloat16)).astype(jnp.float32)
        query_grad = jnp.einsum('gjts,sgd->tgjd', dscores, key_window, precision=highest) * scaling
        return (attended_bf.reshape(TOK_DEV, query_width), query_grad.astype(jnp.bfloat16).reshape(TOK_DEV, query_width), log_total[..., 0], delta_row)
    attended_stack, query_stack, log_stack, delta_stack = lax.map(forward_block, jnp.arange(block_count, dtype=jnp.int32))
    log_padded = jnp.concatenate([log_stack, jnp.zeros((REACH, kv_heads, group_size, TOK_DEV), jnp.float32)], axis=0)
    delta_flat = delta_stack.reshape(TOKENS, kv_heads, group_size)
    delta_padded = jnp.concatenate([delta_flat, jnp.zeros((REACH * TOK_DEV, kv_heads, group_size), jnp.float32)], axis=0)

    def backward_keys(block_index):
        start = (block_index * TOK_DEV).astype(jnp.int32)
        key_block = lax.dynamic_slice_in_dim(key_states, start, TOK_DEV, 0).astype(jnp.float32)
        key_block = key_block.reshape(TOK_DEV, kv_heads, HD)
        value_block = lax.dynamic_slice_in_dim(value_states, start, TOK_DEV, 0).astype(jnp.float32)
        value_block = value_block.reshape(TOK_DEV, kv_heads, HD)
        query_window = lax.dynamic_slice_in_dim(query_padded, start, window, 0).astype(jnp.float32)
        query_window = query_window.reshape(window, kv_heads, group_size, HD)
        grad_window = lax.dynamic_slice_in_dim(grad_padded, start, window, 0).astype(jnp.float32)
        grad_window = grad_window.reshape(window, kv_heads, group_size, HD)
        log_window = lax.dynamic_slice_in_dim(log_padded, block_index, REACH + 1, 0)
        log_window = jnp.transpose(log_window, (1, 2, 0, 3)).reshape(kv_heads, group_size, window)
        delta_window = lax.dynamic_slice_in_dim(delta_padded, start, window, 0)
        delta_window = jnp.transpose(delta_window, (1, 2, 0))
        query_pos = start + jnp.arange(window, dtype=jnp.int32)
        key_pos = start + jnp.arange(TOK_DEV, dtype=jnp.int32)
        allowed = document_of(doc_ends, query_pos)[:, None] == document_of(doc_ends, key_pos)[None, :]
        allowed = allowed & (key_pos[None, :] <= query_pos[:, None]) & (query_pos[:, None] < TOKENS)
        scores = jnp.einsum('tgjd,sgd->gjts', query_window, key_block, precision=highest) * scaling
        scores = jnp.where(allowed[None, None], scores, masked_score)
        probs = jnp.exp(scores - log_window[..., None])
        probs_bf = lax.optimization_barrier(probs.astype(jnp.bfloat16)).astype(jnp.float32)
        dprobs = jnp.einsum('tgjd,sgd->gjts', grad_window, value_block, precision=highest)
        dscores = probs * (dprobs - delta_window[..., None])
        dscores = lax.optimization_barrier(dscores.astype(jnp.bfloat16)).astype(jnp.float32)
        key_grad = jnp.einsum('gjts,tgjd->sgd', dscores, query_window, precision=highest) * scaling
        value_grad = jnp.einsum('gjts,tgjd->sgd', probs_bf, grad_window, precision=highest)
        return (key_grad.astype(jnp.bfloat16).reshape(TOK_DEV, key_width), value_grad.astype(jnp.bfloat16).reshape(TOK_DEV, key_width))
    key_stack, value_stack = lax.map(backward_keys, jnp.arange(block_count, dtype=jnp.int32))
    attended_all = attended_stack.reshape(TOKENS, query_width)
    query_all = query_stack.reshape(TOKENS, query_width)
    key_all = key_stack.reshape(TOKENS, key_width)
    value_all = value_stack.reshape(TOKENS, key_width)
    return (attended_all, query_all, key_all, value_all)
```

```python
import math

import jax
import jax.numpy as jnp
from jax import lax
from jax.experimental import pallas as pl
from jax.experimental.pallas import tpu as pltpu
from jax.sharding import PartitionSpec as P

HD = 128
REACH = 4
MASKED = -1e30
SCALING = 1.0 / math.sqrt(HD)
EXP2_SCALING = SCALING * math.log2(math.e)


def shifted(block, distance):
    axes = ("ctx", "rep")
    devices = range(lax.axis_size(axes))
    route = [(i, i + distance) for i in devices if i + distance in devices]
    return lax.ppermute(block, axes, route)


def contract(a, b, dim_a, dim_b):
    return lax.dot_general(
        a, b, (((dim_a,), (dim_b,)), ((), ())), preferred_element_type=jnp.float32
    )


def attention_kernel(first_ref, lengths_ref, q_ref, g_ref, *refs):
    blocks = REACH + 1
    kv_refs, refs = refs[:blocks], refs[blocks:]
    att_ref, qg_ref, own_ref = refs[:3]
    term_refs = refs[3 : 3 + REACH]
    p_scr, ds_scr = refs[3 + REACH :]
    rows = q_ref.shape[0]
    kv_heads = kv_refs[0].shape[1] // (2 * HD)
    group = q_ref.shape[1] // HD // kv_heads
    keys = blocks * rows
    pair = 2
    cols = pair * rows

    lengths = lengths_ref[...]
    docs = lengths.shape[1]
    upto = lax.broadcasted_iota(jnp.int32, (docs, docs), 1) <= lax.broadcasted_iota(
        jnp.int32, (docs, docs), 0
    )
    ends = jnp.sum(jnp.where(upto, lengths, 0), axis=1, keepdims=True)
    first = first_ref[0]
    pos = first + lax.broadcasted_iota(jnp.int32, (docs, rows), 1)
    begins = jnp.max(jnp.where(ends <= pos, ends, 0), axis=0, keepdims=True)
    low = begins - first + REACH * rows
    high = REACH * rows + lax.broadcasted_iota(jnp.int32, (1, rows), 1)
    low = jnp.concatenate([low] * pair, axis=1)
    high = jnp.concatenate([high] * pair, axis=1)
    key = lax.broadcasted_iota(jnp.int32, (keys, cols), 0)
    allowed = (key >= low) & (key <= high)

    for kv in range(kv_heads):
        k_cols = slice(kv * HD, (kv + 1) * HD)
        v_cols = slice((kv_heads + kv) * HD, (kv_heads + kv + 1) * HD)
        k = jnp.concatenate([r[:, k_cols] for r in kv_refs], axis=0)
        v = jnp.concatenate([r[:, v_cols] for r in kv_refs], axis=0)
        for part in range(group // pair):
            heads = [kv * group + part * pair + h for h in range(pair)]
            q = jnp.concatenate([q_ref[:, h * HD : (h + 1) * HD] for h in heads], axis=0)
            g = jnp.concatenate([g_ref[:, h * HD : (h + 1) * HD] for h in heads], axis=0)
            s = jnp.where(allowed, contract(k, q, 1, 1), MASKED)
            top = jnp.max(s, axis=0, keepdims=True)
            p = jnp.exp2((s - top) * EXP2_SCALING)
            p = p * (1.0 / jnp.sum(p, axis=0, keepdims=True))
            p_bf = p.astype(jnp.bfloat16)
            att = contract(v, p_bf, 0, 0).astype(jnp.bfloat16)
            delta = jnp.sum(
                g.T.astype(jnp.float32) * att.astype(jnp.float32), axis=0, keepdims=True
            )
            ds = (p * (contract(v, g, 1, 1) - delta)).astype(jnp.bfloat16)
            qg = (contract(k, ds, 0, 0) * SCALING).astype(jnp.bfloat16)
            att_t = att.T
            qg_t = qg.T
            for n, h in enumerate(heads):
                att_ref[:, h * HD : (h + 1) * HD] = att_t[n * rows : (n + 1) * rows]
                qg_ref[:, h * HD : (h + 1) * HD] = qg_t[n * rows : (n + 1) * rows]
            p_scr[:, part * cols : (part + 1) * cols] = p_bf
            ds_scr[:, part * cols : (part + 1) * cols] = ds
        heads = [kv * group + h for h in range(group)]
        q = jnp.concatenate([q_ref[:, h * HD : (h + 1) * HD] for h in heads], axis=0)
        g = jnp.concatenate([g_ref[:, h * HD : (h + 1) * HD] for h in heads], axis=0)
        kg = contract(ds_scr[...], q, 1, 0) * SCALING
        vg = contract(p_scr[...], g, 1, 0)
        for n in range(REACH):
            term_refs[n][:, k_cols] = kg[n * rows : (n + 1) * rows].astype(jnp.bfloat16)
            term_refs[n][:, v_cols] = vg[n * rows : (n + 1) * rows].astype(jnp.bfloat16)
        own_ref[:, k_cols] = kg[REACH * rows :]
        own_ref[:, v_cols] = vg[REACH * rows :]


def attention(first, lengths, queries, out_grad, kv_blocks):
    rows, width = queries.shape
    kv_width = kv_blocks[0].shape[1]
    keys = (REACH + 1) * rows
    group_cols = rows * (width // HD) // (kv_width // (2 * HD))
    vmem = pl.BlockSpec(memory_space=pltpu.VMEM)
    term = jax.ShapeDtypeStruct((rows, kv_width), jnp.bfloat16)
    wide = jax.ShapeDtypeStruct((rows, width), jnp.bfloat16)
    flops = 6 * 2 * keys * rows * width
    return pl.pallas_call(
        attention_kernel,
        out_shape=(wide, wide, jax.ShapeDtypeStruct((rows, kv_width), jnp.float32))
        + (term,) * REACH,
        in_specs=[pl.BlockSpec(memory_space=pltpu.SMEM)] + [vmem] * (3 + REACH + 1),
        out_specs=(vmem,) * (3 + REACH),
        scratch_shapes=[
            pltpu.VMEM((keys, group_cols), jnp.bfloat16),
            pltpu.VMEM((keys, group_cols), jnp.bfloat16),
        ],
        compiler_params=pltpu.CompilerParams(vmem_limit_bytes=40 << 20),
        cost_estimate=pl.CostEstimate(
            flops=flops,
            bytes_accessed=8 * rows * width + 24 * rows * kv_width,
            transcendentals=keys * rows * width // HD,
        ),
        name="attention",
    )(first, lengths, queries, out_grad, *kv_blocks)


def per_device(queries, key_states, value_states, out_grad, doc_lengths):
    rows = queries.shape[0]
    width = key_states.shape[1]
    first = (lax.axis_index(("ctx", "rep")) * rows).astype(jnp.int32).reshape(1)
    own = jnp.concatenate([key_states, value_states], axis=1)
    received = [shifted(own, distance) for distance in range(REACH, 0, -1)]
    attended, query_grad, own_terms, *terms = attention(
        first, doc_lengths.reshape(1, -1), queries, out_grad, received + [own]
    )
    total = own_terms
    for distance, term in zip(range(REACH, 0, -1), terms):
        total = total + shifted(term, -distance).astype(jnp.float32)
    total = total.astype(jnp.bfloat16)
    return attended, query_grad, total[:, :width], total[:, width:]


def solution(mesh):
    split = P(("ctx", "rep"), "tp")
    return jax.shard_map(
        per_device,
        mesh=mesh,
        in_specs=(split, split, split, split, P()),
        out_specs=(split, split, split, split),
        check_vma=False,
    )
```

```python
import math

import jax
import jax.numpy as jnp
from jax import lax
from jax.experimental import pallas as pl
from jax.experimental.pallas import tpu as pltpu
from jax.sharding import PartitionSpec as P

HD = 128
REACH = 4
NEAR = 2
HALVES = 2
MASKED = -1e30
SCALING = 1.0 / math.sqrt(HD)
EXP2_SCALING = SCALING * math.log2(math.e)
VMEM = pl.BlockSpec(memory_space=pltpu.VMEM)
HBM = pl.BlockSpec(memory_space=pltpu.MemorySpace.HBM)


def shifted(block, distance):
    axes = ("ctx", "rep")
    devices = range(lax.axis_size(axes))
    route = [(i, i + distance) for i in devices if i + distance in devices]
    return lax.ppermute(block, axes, route)


def contract(a, b, dim_a, dim_b):
    return lax.dot_general(
        a, b, (((dim_a,), (dim_b,)), ((), ())), preferred_element_type=jnp.float32
    )


def call(kernel, name, outs, specs, operands, flops, scratch=()):
    size = lambda a: math.prod(a.shape) * jnp.dtype(a.dtype).itemsize
    return pl.pallas_call(
        kernel,
        out_shape=tuple(outs),
        in_specs=specs,
        out_specs=(VMEM,) * len(outs),
        scratch_shapes=list(scratch),
        compiler_params=pltpu.CompilerParams(vmem_limit_bytes=24 << 20),
        cost_estimate=pl.CostEstimate(
            flops=flops,
            bytes_accessed=sum(map(size, (*operands, *outs))),
            transcendentals=0,
        ),
        name=name,
    )(*operands)


def tile_of(ref, heads, half):
    part = ref.shape[0] // HALVES
    return jnp.concatenate(
        [ref[half * part : (half + 1) * part, h * HD : (h + 1) * HD] for h in heads], axis=0
    )


def key_cols(kv):
    return slice(kv * HD, (kv + 1) * HD)


def value_cols(kv, kv_heads):
    return slice((kv_heads + kv) * HD, (kv_heads + kv + 1) * HD)


def load_kernel(
    first_ref, lengths_hbm, k_hbm, v_hbm, q_hbm, g_hbm, kv_ref, q_ref, g_ref, low_ref, lengths_ref, sems
):
    width = k_hbm.shape[1]
    copies = [
        pltpu.make_async_copy(src, dst, sems.at[n])
        for n, (src, dst) in enumerate(
            [
                (lengths_hbm, lengths_ref),
                (k_hbm, kv_ref.at[:, :width]),
                (v_hbm, kv_ref.at[:, width:]),
                (q_hbm, q_ref),
                (g_hbm, g_ref),
            ]
        )
    ]
    for copy in copies:
        copy.start()
    copies[0].wait()
    rows = q_ref.shape[0]
    lengths = lengths_ref[...]
    docs = lengths.shape[1]
    upto = lax.broadcasted_iota(jnp.int32, (docs, docs), 1) <= lax.broadcasted_iota(
        jnp.int32, (docs, docs), 0
    )
    ends = jnp.sum(jnp.where(upto, lengths, 0), axis=1, keepdims=True)
    first = first_ref[0]
    pos = first + lax.broadcasted_iota(jnp.int32, (docs, rows), 1)
    begins = jnp.max(jnp.where(ends <= pos, ends, 0), axis=0, keepdims=True)
    low = begins - first + REACH * rows
    part = rows // HALVES
    group = low_ref.shape[1] // part
    for half in range(HALVES):
        low_ref[half : half + 1] = jnp.concatenate(
            [low[:, half * part : (half + 1) * part]] * group, axis=1
        )
    for copy in copies[1:]:
        copy.wait()


def near_kernel(low_ref, q_ref, g_ref, *refs):
    kv_refs = refs[NEAR - 1 :: -1] + refs[NEAR : NEAR + 1]
    p_ref, d_ref, stat_ref = refs[NEAR + 1 :]
    rows = q_ref.shape[0]
    part = rows // HALVES
    kv_heads = kv_refs[0].shape[1] // (2 * HD)
    group = q_ref.shape[1] // HD // kv_heads
    cols = group * part
    before = NEAR * rows
    offset = (REACH - NEAR) * rows
    for kv in range(kv_heads):
        heads = range(kv * group, (kv + 1) * group)
        for half in range(HALVES):
            own = (half + 1) * part
            keys = before + own
            k = jnp.concatenate([r[:, key_cols(kv)] for r in kv_refs], axis=0)[:keys]
            v = jnp.concatenate([r[:, value_cols(kv, kv_heads)] for r in kv_refs], axis=0)[:keys]
            q = tile_of(q_ref, heads, half)
            g = tile_of(g_ref, heads, half)
            low = low_ref[half : half + 1]
            query = half * part + lax.broadcasted_iota(jnp.int32, (1, cols), 1) % part
            key = lax.broadcasted_iota(jnp.int32, (before, cols), 0) + offset
            own_key = lax.broadcasted_iota(jnp.int32, (own, cols), 0)
            allowed = jnp.concatenate(
                [key >= low, (own_key + REACH * rows >= low) & (own_key <= query)], axis=0
            )
            s = jnp.where(allowed, contract(k, q, 1, 1), MASKED)
            top = jnp.max(s, axis=0, keepdims=True)
            p = jnp.exp2((s - top) * EXP2_SCALING)
            tile = slice(half * cols, (half + 1) * cols)
            p_ref[kv, :keys, tile] = p
            d_ref[kv, :keys, tile] = contract(v, g, 1, 1)
            stat_ref[kv, 0:1, tile] = top
            stat_ref[kv, 1:2, tile] = jnp.sum(p, axis=0, keepdims=True)


def terms_kernel(low_ref, q_ref, g_ref, p_ref, d_ref, stat_ref, *refs):
    blocks = REACH + 1
    kv_refs, refs = refs[:blocks], refs[blocks:]
    term_refs, (att_ref, ds_ref, own_ref, p_scr) = refs[:REACH], refs[REACH:]
    rows = q_ref.shape[0]
    part = rows // HALVES
    kv_heads = kv_refs[0].shape[1] // (2 * HD)
    group = q_ref.shape[1] // HD // kv_heads
    cols = group * part
    far = REACH - NEAR
    split = far * rows
    for kv in range(kv_heads):
        heads = range(kv * group, (kv + 1) * group)
        k = jnp.concatenate([r[:, key_cols(kv)] for r in kv_refs[:far]], axis=0)
        v = jnp.concatenate([r[:, value_cols(kv, kv_heads)] for r in kv_refs], axis=0)
        qs, gs = [], []
        for half in range(HALVES):
            start = half * part
            stop = REACH * rows + (half + 1) * part
            q = tile_of(q_ref, heads, half)
            g = tile_of(g_ref, heads, half)
            qs.append(q)
            gs.append(g)
            tile = slice(half * cols, (half + 1) * cols)
            low = low_ref[half : half + 1]
            key = lax.broadcasted_iota(jnp.int32, (split - start, cols), 0) + start
            s = jnp.where(key >= low, contract(k[start:], q, 1, 1), MASKED)
            near_top = stat_ref[kv, 0:1, tile]
            top = jnp.maximum(near_top, jnp.max(s, axis=0, keepdims=True))
            p = jnp.exp2((s - top) * EXP2_SCALING)
            ratio = jnp.exp2((near_top - top) * EXP2_SCALING)
            total = ratio * stat_ref[kv, 1:2, tile] + jnp.sum(p, axis=0, keepdims=True)
            inverse = 1.0 / total
            p = p * inverse
            p_near = p_ref[kv, : stop - split, tile] * (ratio * inverse)
            p_bf = jnp.concatenate([p.astype(jnp.bfloat16), p_near.astype(jnp.bfloat16)], axis=0)
            att = contract(v[start:stop], p_bf, 0, 0).astype(jnp.bfloat16)
            delta = jnp.sum(
                g.T.astype(jnp.float32) * att.astype(jnp.float32), axis=0, keepdims=True
            )
            ds = p * (contract(v[start:split], g, 1, 1) - delta)
            ds_near = p_near * (d_ref[kv, : stop - split, tile] - delta)
            att_ref[kv, :, tile] = att
            p_scr[start:stop, tile] = p_bf
            ds_ref[kv, start:split, tile] = ds.astype(jnp.bfloat16)
            ds_ref[kv, split:stop, tile] = ds_near.astype(jnp.bfloat16)
            rest = slice(0, start) if half else slice(stop, blocks * rows)
            p_scr[rest, tile] = jnp.zeros((part, cols), jnp.bfloat16)
            ds_ref[kv, rest, tile] = jnp.zeros((part, cols), jnp.bfloat16)
        remote = REACH * rows
        kg = contract(ds_ref[kv, :remote], jnp.concatenate(qs, axis=0), 1, 0) * SCALING
        vg = contract(p_scr[:remote], jnp.concatenate(gs, axis=0), 1, 0)
        for n in range(REACH):
            block = slice(n * rows, (n + 1) * rows)
            term_refs[n][:, key_cols(kv)] = kg[block].astype(jnp.bfloat16)
            term_refs[n][:, value_cols(kv, kv_heads)] = vg[block].astype(jnp.bfloat16)
        own_ref[kv] = p_scr[remote:]


def own_kernel(q_ref, g_ref, att_ref, ds_ref, own_ref, *refs):
    kv_refs = refs[: REACH + 1]
    att_out, qg_out, total_ref = refs[REACH + 1 :]
    rows = q_ref.shape[0]
    part = rows // HALVES
    kv_heads = kv_refs[0].shape[1] // (2 * HD)
    group = q_ref.shape[1] // HD // kv_heads
    cols = group * part
    remote = REACH * rows
    for kv in range(kv_heads):
        heads = range(kv * group, (kv + 1) * group)
        k = jnp.concatenate([r[:, key_cols(kv)] for r in kv_refs], axis=0)
        q = jnp.concatenate([tile_of(q_ref, heads, half) for half in range(HALVES)], axis=0)
        g = jnp.concatenate([tile_of(g_ref, heads, half) for half in range(HALVES)], axis=0)
        total_ref[:, key_cols(kv)] = contract(ds_ref[kv, remote:], q, 1, 0) * SCALING
        total_ref[:, value_cols(kv, kv_heads)] = contract(own_ref[kv], g, 1, 0)
        for half in range(HALVES):
            tile = slice(half * cols, (half + 1) * cols)
            start = half * part
            stop = remote + (half + 1) * part
            qg = contract(k[start:stop], ds_ref[kv, start:stop, tile], 0, 0) * SCALING
            qg = qg.astype(jnp.bfloat16).T
            att = att_ref[kv, :, tile].T
            for n, h in enumerate(heads):
                out = (slice(start, start + part), slice(h * HD, (h + 1) * HD))
                att_out[out] = att[n * part : (n + 1) * part]
                qg_out[out] = qg[n * part : (n + 1) * part]


def add_kernel(total_ref, *refs):
    term_refs, (k_ref, v_ref) = refs[:REACH], refs[REACH:]
    width = k_ref.shape[1]
    total = total_ref[...]
    for term_ref in term_refs:
        total = total + term_ref[...].astype(jnp.float32)
    k_ref[...] = total[:, :width].astype(jnp.bfloat16)
    v_ref[...] = total[:, width:].astype(jnp.bfloat16)


def per_device(queries, key_states, value_states, out_grad, doc_lengths):
    rows, width = queries.shape
    kv_width = 2 * key_states.shape[1]
    kv_heads = kv_width // (2 * HD)
    group = width // HD // kv_heads
    half_cols = group * rows // HALVES
    cols = group * rows
    near_keys = (NEAR + 1) * rows
    keys = (REACH + 1) * rows
    bf16, f32 = jnp.bfloat16, jnp.float32
    array = jax.ShapeDtypeStruct
    narrow = array((rows, kv_width), bf16)
    wide = array((rows, width), bf16)
    first = (lax.axis_index(("ctx", "rep")) * rows).astype(jnp.int32).reshape(1)
    own, q, g, low = call(
        load_kernel,
        "load",
        [narrow, wide, wide, array((HALVES, half_cols), jnp.int32)],
        [pl.BlockSpec(memory_space=pltpu.SMEM)] + [HBM] * 5,
        [first]
        + [
            pltpu.with_memory_space_constraint(a, pltpu.MemorySpace.HBM)
            for a in (doc_lengths.reshape(1, -1), key_states, value_states, queries, out_grad)
        ],
        0,
        [pltpu.VMEM((1, doc_lengths.shape[0]), jnp.int32), pltpu.SemaphoreType.DMA((5,))],
    )
    received = {distance: shifted(own, distance) for distance in (4, 3, 1, 2)}
    blocks = [received[distance] for distance in range(REACH, 0, -1)] + [own]
    work = 2 * HD * rows * cols * kv_heads
    p, d, stat = call(
        near_kernel,
        "near",
        [array((kv_heads, near_keys, cols), f32)] * 2 + [array((kv_heads, 2, cols), f32)],
        [VMEM] * (4 + NEAR),
        [low, q, g] + blocks[REACH - 1 : REACH - NEAR - 1 : -1] + [own],
        2 * (NEAR + 1) * work,
    )
    *terms, att, ds, own_p = call(
        terms_kernel,
        "terms",
        [narrow] * REACH
        + [
            array((kv_heads, HD, cols), bf16),
            array((kv_heads, keys, cols), bf16),
            array((kv_heads, rows, cols), bf16),
        ],
        [VMEM] * (7 + REACH),
        [low, q, g, p, d, stat] + blocks,
        (3 * REACH + 5) * work,
        [pltpu.VMEM((keys, cols), bf16)],
    )
    returned = {distance: shifted(terms[REACH - distance], -distance) for distance in (2, 1, 3, 4)}
    attended, query_grad, total = call(
        own_kernel,
        "own",
        [wide, wide, array((rows, kv_width), f32)],
        [VMEM] * (6 + REACH),
        [q, g, att, ds, own_p] + blocks,
        (REACH + 3) * work,
    )
    key_grad, value_grad = call(
        add_kernel,
        "add",
        [array(key_states.shape, bf16)] * 2,
        [VMEM] * (1 + REACH),
        [total] + list(returned.values()),
        0,
    )
    return attended, query_grad, key_grad, value_grad


def solution(mesh):
    split = P(("ctx", "rep"), "tp")
    return jax.shard_map(
        per_device,
        mesh=mesh,
        in_specs=(split, split, split, split, P()),
        out_specs=(split, split, split, split),
        check_vma=False,
    )
```

```python
import math

import jax
import jax.numpy as jnp
from jax import lax
from jax.experimental import pallas as pl
from jax.experimental.pallas import tpu as pltpu
from jax.sharding import PartitionSpec as P

HD = 128
REACH = 4
ORDER = (4, 3, 1, 2, 0)
FAR = 3
HALVES = 2
MASKED = -1e30
SCALING = 1.0 / math.sqrt(HD)
EXP2_SCALING = SCALING * math.log2(math.e)
VMEM = pl.BlockSpec(memory_space=pltpu.VMEM)
HBM = pl.BlockSpec(memory_space=pltpu.MemorySpace.HBM)


def shifted(block, distance):
    axes = ("ctx", "rep")
    devices = range(lax.axis_size(axes))
    route = [(i, i + distance) for i in devices if i + distance in devices]
    return lax.ppermute(block, axes, route)


def contract(a, b, dim_a, dim_b):
    return lax.dot_general(
        a, b, (((dim_a,), (dim_b,)), ((), ())), preferred_element_type=jnp.float32
    )


def call(kernel, name, outs, specs, operands, flops, scratch=()):
    size = lambda a: math.prod(a.shape) * jnp.dtype(a.dtype).itemsize
    return pl.pallas_call(
        kernel,
        out_shape=tuple(outs),
        in_specs=specs,
        out_specs=(VMEM,) * len(outs),
        scratch_shapes=list(scratch),
        compiler_params=pltpu.CompilerParams(vmem_limit_bytes=24 << 20),
        cost_estimate=pl.CostEstimate(
            flops=flops,
            bytes_accessed=sum(map(size, (*operands, *outs))),
            transcendentals=0,
        ),
        name=name,
    )(*operands)


def window(distance):
    return ORDER.index(distance)


def key_cols(kv):
    return slice(kv * HD, (kv + 1) * HD)


def value_cols(kv, kv_heads):
    return slice((kv_heads + kv) * HD, (kv_heads + kv + 1) * HD)


def join_kernel(k_hbm, v_hbm, kv_ref, sems):
    width = k_hbm.shape[1]
    copies = [
        pltpu.make_async_copy(k_hbm, kv_ref.at[:, :width], sems.at[0]),
        pltpu.make_async_copy(v_hbm, kv_ref.at[:, width:], sems.at[1]),
    ]
    for copy in copies:
        copy.start()
    for copy in copies:
        copy.wait()


def load_kernel(
    first_ref, lengths_hbm, q_hbm, g_hbm, q_ref, g_ref, qt_ref, gt_ref, low_ref, *scratch
):
    lengths_ref, q_scr, g_scr, sems = scratch
    copies = [
        pltpu.make_async_copy(lengths_hbm, lengths_ref, sems.at[0]),
        pltpu.make_async_copy(q_hbm, q_scr, sems.at[1]),
        pltpu.make_async_copy(g_hbm, g_scr, sems.at[2]),
    ]
    for copy in copies:
        copy.start()
    copies[0].wait()
    rows = q_scr.shape[0]
    kv_heads, cols = q_ref.shape[:2]
    group = cols // rows
    part = rows // HALVES
    lengths = lengths_ref[...]
    docs = lengths.shape[1]
    upto = lax.broadcasted_iota(jnp.int32, (docs, docs), 1) <= lax.broadcasted_iota(
        jnp.int32, (docs, docs), 0
    )
    ends = jnp.sum(jnp.where(upto, lengths, 0), axis=1, keepdims=True)
    first = first_ref[0]
    pos = first + lax.broadcasted_iota(jnp.int32, (docs, rows), 1)
    begins = jnp.max(jnp.where(ends <= pos, ends, 0), axis=0, keepdims=True)
    low = begins - first + REACH * rows
    for half in range(HALVES):
        low_ref[half : half + 1] = jnp.concatenate(
            [low[:, half * part : (half + 1) * part]] * group, axis=1
        )
    for copy, scr, ref, t_ref in (
        (copies[1], q_scr, q_ref, qt_ref),
        (copies[2], g_scr, g_ref, gt_ref),
    ):
        copy.wait()
        for kv in range(kv_heads):
            tall = jnp.concatenate(
                [
                    scr[half * part : (half + 1) * part, h * HD : (h + 1) * HD]
                    for half in range(HALVES)
                    for h in range(kv * group, (kv + 1) * group)
                ],
                axis=0,
            )
            ref[kv] = tall
            t_ref[kv] = tall.T


def own_rows(rows, half):
    return (half + 1) * (rows // HALVES)


def keys_of(distances, rows, cols, skip=0):
    places = [
        lax.broadcasted_iota(jnp.int32, (rows, cols), 0) + (REACH - distance) * rows
        for distance in distances
    ]
    return jnp.concatenate(places, axis=0)[skip:]


def near_kernel(low_ref, qt_ref, gt_ref, *refs):
    kv_refs, (p_ref, d_ref, stat_ref) = refs[:-3], refs[-3:]
    rows = kv_refs[0].shape[0]
    kv_heads, _, all_cols = qt_ref.shape
    cols = all_cols // HALVES
    part = rows // HALVES
    before = (len(kv_refs) - 1) * rows
    for kv in range(kv_heads):
        for half in range(HALVES):
            own = own_rows(rows, half)
            keys = before + own
            tile = slice(half * cols, (half + 1) * cols)
            k = jnp.concatenate([r[:, key_cols(kv)] for r in kv_refs], axis=0)[:keys]
            v = jnp.concatenate([r[:, value_cols(kv, kv_heads)] for r in kv_refs], axis=0)[:keys]
            low = low_ref[half : half + 1]
            query = half * part + lax.broadcasted_iota(jnp.int32, (1, cols), 1) % part
            own_key = lax.broadcasted_iota(jnp.int32, (own, cols), 0)
            allowed = jnp.concatenate(
                [
                    keys_of(ORDER[FAR:-1], rows, cols) >= low,
                    (own_key + REACH * rows >= low) & (own_key <= query),
                ],
                axis=0,
            )
            s = jnp.where(allowed, contract(k, qt_ref[kv, :, tile], 1, 0), MASKED)
            top = jnp.max(s, axis=0, keepdims=True)
            p = jnp.exp2((s - top) * EXP2_SCALING)
            p_ref[kv, :keys, tile] = p
            d_ref[kv, :keys, tile] = contract(v, gt_ref[kv, :, tile], 1, 0)
            stat_ref[kv, 0:1, tile] = top
            stat_ref[kv, 1:2, tile] = jnp.sum(p, axis=0, keepdims=True)


def terms_kernel(low_ref, q_ref, g_ref, qt_ref, gt_ref, p_near_ref, d_near_ref, stat_ref, *refs):
    blocks = REACH + 1
    kv_refs, refs = refs[:blocks], refs[blocks:]
    term_refs, (att_ref, p_ref, ds_ref, p_scr, d_scr) = refs[:REACH], refs[REACH:]
    rows = kv_refs[0].shape[0]
    kv_heads, _, all_cols = qt_ref.shape
    cols = all_cols // HALVES
    part = rows // HALVES
    split = FAR * rows

    def kept(n, half):
        start = half * part if n == 0 else 0
        stop = own_rows(rows, half) if n == REACH else rows
        return slice(n * rows + start, n * rows + stop)

    def probs(kv, n, half):
        tile = slice(half * cols, (half + 1) * cols)
        here = kept(n, half)
        if n < FAR:
            return p_scr[kv, here, tile], d_scr[kv, here, tile]
        near = slice(here.start - split, here.stop - split)
        return p_near_ref[kv, near, tile], d_near_ref[kv, near, tile]

    def scores(kv, half):
        start = half * part
        tile = slice(half * cols, (half + 1) * cols)
        k = jnp.concatenate([r[:, key_cols(kv)] for r in kv_refs[:FAR]], axis=0)[start:]
        v = jnp.concatenate([r[:, value_cols(kv, kv_heads)] for r in kv_refs[:FAR]], axis=0)[start:]
        allowed = keys_of(ORDER[:FAR], rows, cols, start) >= low_ref[half : half + 1]
        s = jnp.where(allowed, contract(k, qt_ref[kv, :, tile], 1, 0), MASKED)
        near_top = stat_ref[kv, 0:1, tile]
        top = jnp.maximum(near_top, jnp.max(s, axis=0, keepdims=True))
        p = jnp.exp2((s - top) * EXP2_SCALING)
        p_scr[kv, start:split, tile] = p
        d_scr[kv, start:split, tile] = contract(v, gt_ref[kv, :, tile], 1, 0)
        ratio = jnp.exp2((near_top - top) * EXP2_SCALING)
        total = ratio * stat_ref[kv, 1:2, tile] + jnp.sum(p, axis=0, keepdims=True)
        inverse = 1.0 / total
        return inverse, ratio * inverse

    def attend(kv, half, scales):
        tile = slice(half * cols, (half + 1) * cols)
        att = jnp.zeros((HD, cols), jnp.float32)
        for n in range(blocks):
            here = kept(n, half)
            v = kv_refs[n][here.start - n * rows : here.stop - n * rows, value_cols(kv, kv_heads)]
            p_bf = (probs(kv, n, half)[0] * scales[n >= FAR]).astype(jnp.bfloat16)
            p_ref[kv, here, tile] = p_bf
            att = att + contract(v, p_bf, 0, 0)
        att = att.astype(jnp.bfloat16)
        att_ref[kv, :, tile] = att
        gt = gt_ref[kv, :, tile].astype(jnp.float32)
        return jnp.sum(gt * att.astype(jnp.float32), axis=0, keepdims=True)

    def send(kv, n, scales, deltas):
        for half in range(HALVES):
            tile = slice(half * cols, (half + 1) * cols)
            p, d = probs(kv, n, half)
            ds = (p * scales[half][n >= FAR]) * (d - deltas[half])
            ds_ref[kv, kept(n, half), tile] = ds.astype(jnp.bfloat16)
        if n < REACH:
            block = slice(n * rows, (n + 1) * rows)
            kg = contract(ds_ref[kv, block], q_ref[kv], 1, 0) * SCALING
            vg = contract(p_ref[kv, block], g_ref[kv], 1, 0)
            term_refs[n][:, key_cols(kv)] = kg.astype(jnp.bfloat16)
            term_refs[n][:, value_cols(kv, kv_heads)] = vg.astype(jnp.bfloat16)

    empty = jnp.zeros((part, cols), jnp.bfloat16)
    for kv in range(kv_heads):
        for ref in (p_ref, ds_ref):
            ref[kv, :part, cols:] = empty
            ref[kv, (blocks * rows - part) :, :cols] = empty
    scales = [[scores(kv, half) for half in range(HALVES)] for kv in range(kv_heads)]
    deltas = [[attend(kv, half, scales[kv][half]) for half in range(HALVES)] for kv in range(kv_heads)]
    for kv in range(kv_heads):
        for n in range(blocks):
            send(kv, n, scales[kv], deltas[kv])


def own_kernel(q_ref, g_ref, att_ref, p_ref, ds_ref, *refs):
    kv_refs, (att_out, qg_out, total_ref) = refs[:-3], refs[-3:]
    rows = kv_refs[0].shape[0]
    kv_heads, all_cols = q_ref.shape[:2]
    group = all_cols // rows
    cols = all_cols // HALVES
    part = rows // HALVES
    remote = REACH * rows
    for kv in range(kv_heads):
        k = jnp.concatenate([r[:, key_cols(kv)] for r in kv_refs], axis=0)
        total_ref[:, key_cols(kv)] = contract(ds_ref[kv, remote:], q_ref[kv], 1, 0) * SCALING
        total_ref[:, value_cols(kv, kv_heads)] = contract(p_ref[kv, remote:], g_ref[kv], 1, 0)
        for half in range(HALVES):
            tile = slice(half * cols, (half + 1) * cols)
            start = half * part
            stop = remote + own_rows(rows, half)
            qg = contract(k[start:stop], ds_ref[kv, start:stop, tile], 0, 0) * SCALING
            qg = qg.astype(jnp.bfloat16).T
            att = att_ref[kv, :, tile].T
            for n in range(group):
                h = kv * group + n
                out = (slice(start, start + part), slice(h * HD, (h + 1) * HD))
                att_out[out] = att[n * part : (n + 1) * part]
                qg_out[out] = qg[n * part : (n + 1) * part]


def add_kernel(total_ref, *refs):
    term_refs, (k_ref, v_ref) = refs[:REACH], refs[REACH:]
    width = k_ref.shape[1]
    total = total_ref[...]
    for term_ref in term_refs:
        total = total + term_ref[...].astype(jnp.float32)
    k_ref[...] = total[:, :width].astype(jnp.bfloat16)
    v_ref[...] = total[:, width:].astype(jnp.bfloat16)


def per_device(queries, key_states, value_states, out_grad, doc_lengths):
    rows, width = queries.shape
    kv_width = 2 * key_states.shape[1]
    kv_heads = kv_width // (2 * HD)
    cols = rows * (width // HD // kv_heads)
    near_keys = (REACH + 1 - FAR) * rows
    keys = (REACH + 1) * rows
    bf16, f32 = jnp.bfloat16, jnp.float32
    array = jax.ShapeDtypeStruct
    narrow = array((rows, kv_width), bf16)
    wide = array((rows, width), bf16)
    tall = array((kv_heads, cols, HD), bf16)
    turned = array((kv_heads, HD, cols), bf16)
    scores = array((kv_heads, keys, cols), bf16)
    near_scores = array((kv_heads, near_keys, cols), f32)
    dma = pltpu.SemaphoreType.DMA
    work = 2 * HD * rows * cols * kv_heads
    first = (lax.axis_index(("ctx", "rep")) * rows).astype(jnp.int32).reshape(1)
    in_hbm = lambda a: pltpu.with_memory_space_constraint(a, pltpu.MemorySpace.HBM)

    (own,) = call(
        join_kernel,
        "join",
        [narrow],
        [HBM] * 2,
        [in_hbm(key_states), in_hbm(value_states)],
        0,
        [dma((2,))],
    )
    received = {distance: shifted(own, distance) for distance in (4, 3, 1, 2)}
    q, g, qt, gt, low = call(
        load_kernel,
        "load",
        [tall, tall, turned, turned, array((HALVES, cols // HALVES), jnp.int32)],
        [pl.BlockSpec(memory_space=pltpu.SMEM)] + [HBM] * 3,
        [first, in_hbm(doc_lengths.reshape(1, -1)), in_hbm(queries), in_hbm(out_grad)],
        0,
        [
            pltpu.VMEM((1, doc_lengths.shape[0]), jnp.int32),
            pltpu.VMEM(queries.shape, bf16),
            pltpu.VMEM(out_grad.shape, bf16),
            dma((3,)),
        ],
    )
    blocks = [received[distance] if distance else own for distance in ORDER]
    p, d, stat = call(
        near_kernel,
        "near",
        [near_scores, near_scores, array((kv_heads, 2, cols), f32)],
        [VMEM] * (4 + REACH - FAR),
        [low, qt, gt] + blocks[FAR:],
        2 * (REACH + 1 - FAR) * work,
    )
    *terms, att, p, ds = call(
        terms_kernel,
        "terms",
        [narrow] * REACH + [turned, scores, scores],
        [VMEM] * (9 + REACH),
        [low, q, g, qt, gt, p, d, stat] + blocks,
        (2 * FAR + 3 * REACH + 1) * work,
        [pltpu.VMEM((kv_heads, FAR * rows, cols), f32)] * 2,
    )
    returned = [shifted(terms[window(distance)], -distance) for distance in (2, 1, 3, 4)]
    attended, query_grad, total = call(
        own_kernel,
        "own",
        [wide, wide, array((rows, kv_width), f32)],
        [VMEM] * (6 + REACH),
        [q, g, att, p, ds] + blocks,
        (REACH + 3) * work,
    )
    key_grad, value_grad = call(
        add_kernel,
        "add",
        [array(key_states.shape, bf16)] * 2,
        [VMEM] * (1 + REACH),
        [total] + returned,
        0,
    )
    return attended, query_grad, key_grad, value_grad


def solution(mesh):
    split = P(("ctx", "rep"), "tp")
    return jax.shard_map(
        per_device,
        mesh=mesh,
        in_specs=(split, split, split, split, P()),
        out_specs=(split, split, split, split),
        check_vma=False,
    )
```

```python
import functools
import math

import jax
import jax.numpy as jnp
from jax import lax
from jax.experimental import pallas as pl
from jax.experimental.pallas import tpu as pltpu
from jax.sharding import PartitionSpec as P

HD = 128
REACH = 4
ORDER = (4, 3, 1, 2, 0)
FAR, MID = 2, 1
HALVES = 2
MASKED = -1e30
SCALING = 1.0 / math.sqrt(HD)
EXP2_SCALING = SCALING * math.log2(math.e)
VMEM = pl.BlockSpec(memory_space=pltpu.VMEM)
HBM = pl.BlockSpec(memory_space=pltpu.MemorySpace.HBM)


def shifted(block, distance):
    axes = ("ctx", "rep")
    devices = range(lax.axis_size(axes))
    route = [(i, i + distance) for i in devices if i + distance in devices]
    return lax.ppermute(block, axes, route)


def contract(a, b, dim_a, dim_b):
    return lax.dot_general(
        a, b, (((dim_a,), (dim_b,)), ((), ())), preferred_element_type=jnp.float32
    )


def call(kernel, name, outs, specs, operands, flops, scratch=()):
    size = lambda a: math.prod(a.shape) * jnp.dtype(a.dtype).itemsize
    return pl.pallas_call(
        kernel,
        out_shape=tuple(outs),
        in_specs=specs,
        out_specs=(VMEM,) * len(outs),
        scratch_shapes=list(scratch),
        compiler_params=pltpu.CompilerParams(vmem_limit_bytes=24 << 20),
        cost_estimate=pl.CostEstimate(
            flops=flops,
            bytes_accessed=sum(map(size, (*operands, *outs))),
            transcendentals=0,
        ),
        name=name,
    )(*operands)


def window(distance):
    return ORDER.index(distance)


def key_cols(kv):
    return slice(kv * HD, (kv + 1) * HD)


def value_cols(kv, kv_heads):
    return slice((kv_heads + kv) * HD, (kv_heads + kv + 1) * HD)


def join_kernel(k_hbm, v_hbm, kv_ref, sems):
    width = k_hbm.shape[1]
    copies = [
        pltpu.make_async_copy(k_hbm, kv_ref.at[:, :width], sems.at[0]),
        pltpu.make_async_copy(v_hbm, kv_ref.at[:, width:], sems.at[1]),
    ]
    for copy in copies:
        copy.start()
    for copy in copies:
        copy.wait()


def load_kernel(
    first_ref, lengths_hbm, q_hbm, g_hbm, q_ref, g_ref, qt_ref, gt_ref, low_ref, *scratch
):
    lengths_ref, q_scr, g_scr, sems = scratch
    copies = [
        pltpu.make_async_copy(lengths_hbm, lengths_ref, sems.at[0]),
        pltpu.make_async_copy(q_hbm, q_scr, sems.at[1]),
        pltpu.make_async_copy(g_hbm, g_scr, sems.at[2]),
    ]
    for copy in copies:
        copy.start()
    copies[0].wait()
    rows = q_scr.shape[0]
    kv_heads, cols = q_ref.shape[:2]
    group = cols // rows
    part = rows // HALVES
    lengths = lengths_ref[...]
    docs = lengths.shape[1]
    upto = lax.broadcasted_iota(jnp.int32, (docs, docs), 1) <= lax.broadcasted_iota(
        jnp.int32, (docs, docs), 0
    )
    ends = jnp.sum(jnp.where(upto, lengths, 0), axis=1, keepdims=True)
    first = first_ref[0]
    pos = first + lax.broadcasted_iota(jnp.int32, (docs, rows), 1)
    begins = jnp.max(jnp.where(ends <= pos, ends, 0), axis=0, keepdims=True)
    low = begins - first + REACH * rows
    for half in range(HALVES):
        low_ref[half : half + 1] = jnp.concatenate(
            [low[:, half * part : (half + 1) * part]] * group, axis=1
        )
    for copy, scr, ref, t_ref in (
        (copies[1], q_scr, q_ref, qt_ref),
        (copies[2], g_scr, g_ref, gt_ref),
    ):
        copy.wait()
        for kv in range(kv_heads):
            tall = jnp.concatenate(
                [
                    scr[half * part : (half + 1) * part, h * HD : (h + 1) * HD]
                    for half in range(HALVES)
                    for h in range(kv * group, (kv + 1) * group)
                ],
                axis=0,
            )
            ref[kv] = tall
            t_ref[kv] = tall.T


def own_rows(rows, half):
    return (half + 1) * (rows // HALVES)


def keys_of(distances, rows, cols, skip=0):
    places = [
        lax.broadcasted_iota(jnp.int32, (rows, cols), 0) + (REACH - distance) * rows
        for distance in distances
    ]
    return jnp.concatenate(places, axis=0)[skip:]


def partial_kernel(low_ref, qt_ref, gt_ref, *refs, distances):
    before, kv_refs = refs[: len(refs) - 3 - len(distances)], refs[-3 - len(distances) : -3]
    p_ref, d_ref, stat_ref = refs[-3:]
    rows = kv_refs[0].shape[0]
    kv_heads, _, all_cols = qt_ref.shape
    cols = all_cols // HALVES
    part = rows // HALVES
    for kv in range(kv_heads):
        for half in range(HALVES):
            low = low_ref[half : half + 1]
            own = own_rows(rows, half)
            query = half * part + lax.broadcasted_iota(jnp.int32, (1, cols), 1) % part
            own_key = lax.broadcasted_iota(jnp.int32, (own, cols), 0)
            allowed = jnp.concatenate(
                [
                    keys_of([distance], rows, cols) >= low
                    if distance
                    else (own_key + REACH * rows >= low) & (own_key <= query)
                    for distance in distances
                ],
                axis=0,
            )
            keys = allowed.shape[0]
            tile = slice(half * cols, (half + 1) * cols)
            k = jnp.concatenate([r[:, key_cols(kv)] for r in kv_refs], axis=0)[:keys]
            v = jnp.concatenate([r[:, value_cols(kv, kv_heads)] for r in kv_refs], axis=0)[:keys]
            s = jnp.where(allowed, contract(k, qt_ref[kv, :, tile], 1, 0), MASKED)
            top = jnp.max(s, axis=0, keepdims=True)
            for ref in before:
                top = jnp.maximum(top, ref[kv, 0:1, tile])
            p = jnp.exp2((s - top) * EXP2_SCALING)
            total = jnp.sum(p, axis=0, keepdims=True)
            for ref in before:
                ratio = jnp.exp2((ref[kv, 0:1, tile] - top) * EXP2_SCALING)
                total = total + ratio * ref[kv, 1:2, tile]
                stat_ref[kv, 2:3, tile] = ratio
            p_ref[kv, :keys, tile] = p
            d_ref[kv, :keys, tile] = contract(v, gt_ref[kv, :, tile], 1, 0)
            stat_ref[kv, 0:1, tile] = top
            stat_ref[kv, 1:2, tile] = total


def terms_kernel(low_ref, q_ref, g_ref, qt_ref, gt_ref, *refs):
    blocks = REACH + 1
    (p_mid_ref, d_mid_ref, mid_ref, p_near_ref, d_near_ref), refs = refs[:5], refs[5:]
    kv_refs, refs = refs[:blocks], refs[blocks:]
    term_refs, (att_ref, p_ref, ds_ref, row_ref, p_scr, d_scr) = refs[:REACH], refs[REACH:]
    rows = kv_refs[0].shape[0]
    kv_heads, _, all_cols = qt_ref.shape
    cols = all_cols // HALVES
    part = rows // HALVES
    group_of = [0] * FAR + [1] * MID + [2] * (blocks - FAR - MID)
    firsts = [0, FAR, FAR + MID]
    sources = [(p_scr, d_scr), (p_mid_ref, d_mid_ref), (p_near_ref, d_near_ref)]

    def kept(n, half, base=0):
        start = half * part if n == 0 else 0
        stop = own_rows(rows, half) if n == REACH else rows
        return slice((n - base) * rows + start, (n - base) * rows + stop)

    def held(kv, n, half, which):
        group = group_of[n]
        tile = slice(half * cols, (half + 1) * cols)
        return sources[group][which][kv, kept(n, half, firsts[group]), tile]

    def scores(kv, half):
        start = half * part
        tile = slice(half * cols, (half + 1) * cols)
        k = jnp.concatenate([r[:, key_cols(kv)] for r in kv_refs[:FAR]], axis=0)[start:]
        v = jnp.concatenate([r[:, value_cols(kv, kv_heads)] for r in kv_refs[:FAR]], axis=0)[start:]
        allowed = keys_of(ORDER[:FAR], rows, cols, start) >= low_ref[half : half + 1]
        s = jnp.where(allowed, contract(k, qt_ref[kv, :, tile], 1, 0), MASKED)
        mid_top, mid_sum = mid_ref[kv, 0:1, tile], mid_ref[kv, 1:2, tile]
        top = jnp.maximum(mid_top, jnp.max(s, axis=0, keepdims=True))
        p = jnp.exp2((s - top) * EXP2_SCALING)
        p_scr[kv, start : FAR * rows, tile] = p
        d_scr[kv, start : FAR * rows, tile] = contract(v, gt_ref[kv, :, tile], 1, 0)
        mid = jnp.exp2((mid_top - top) * EXP2_SCALING)
        inverse = 1.0 / (mid * mid_sum + jnp.sum(p, axis=0, keepdims=True))
        mid = mid * inverse
        near = mid * mid_ref[kv, 2:3, tile]
        row_ref[kv, 0:1, tile] = near
        return inverse, mid, near

    def attend(kv, half, scales):
        tile = slice(half * cols, (half + 1) * cols)
        parts, v = [], []
        for n in range(blocks):
            p_bf = (held(kv, n, half, 0) * scales[group_of[n]]).astype(jnp.bfloat16)
            p_ref[kv, kept(n, half), tile] = p_bf
            parts.append(p_bf)
            v.append(kv_refs[n][kept(n, half, n), value_cols(kv, kv_heads)])
        att = contract(jnp.concatenate(v, axis=0), jnp.concatenate(parts, axis=0), 0, 0)
        att = att.astype(jnp.bfloat16)
        att_ref[kv, :, tile] = att
        gt = gt_ref[kv, :, tile].astype(jnp.float32)
        delta = jnp.sum(gt * att.astype(jnp.float32), axis=0, keepdims=True)
        row_ref[kv, 1:2, tile] = delta
        return delta

    def score_grads(kv, half, scales, delta):
        tile = slice(half * cols, (half + 1) * cols)
        for n in range(REACH):
            ds = (held(kv, n, half, 0) * scales[group_of[n]]) * (held(kv, n, half, 1) - delta)
            ds_ref[kv, kept(n, half), tile] = ds.astype(jnp.bfloat16)

    def send(kv):
        kg = contract(ds_ref[kv], q_ref[kv], 1, 0) * SCALING
        vg = contract(p_ref[kv, : REACH * rows], g_ref[kv], 1, 0)
        for n in range(REACH):
            block = slice(n * rows, (n + 1) * rows)
            term_refs[n][:, key_cols(kv)] = kg[block].astype(jnp.bfloat16)
            term_refs[n][:, value_cols(kv, kv_heads)] = vg[block].astype(jnp.bfloat16)

    empty = jnp.zeros((part, cols), jnp.bfloat16)
    for kv in range(kv_heads):
        ds_ref[kv, :part, cols:] = empty
        p_ref[kv, :part, cols:] = empty
        p_ref[kv, (blocks * rows - part) :, :cols] = empty
        scales = [scores(kv, half) for half in range(HALVES)]
        deltas = [attend(kv, half, scales[half]) for half in range(HALVES)]
        for half in range(HALVES):
            score_grads(kv, half, scales[half], deltas[half])
        send(kv)


def own_kernel(q_ref, g_ref, att_ref, p_ref, ds_ref, row_ref, p_near_ref, d_near_ref, *refs):
    kv_refs, (att_out, qg_out, total_ref, own_scr) = refs[:-4], refs[-4:]
    rows = kv_refs[0].shape[0]
    kv_heads, all_cols = q_ref.shape[:2]
    group = all_cols // rows
    cols = all_cols // HALVES
    part = rows // HALVES
    remote = REACH * rows
    own_scr[own_rows(rows, 0) :, :cols] = jnp.zeros((rows - part, cols), jnp.bfloat16)
    for kv in range(kv_heads):
        k = jnp.concatenate([r[:, key_cols(kv)] for r in kv_refs], axis=0)
        for half in range(HALVES):
            tile = slice(half * cols, (half + 1) * cols)
            start = half * part
            own = own_rows(rows, half)
            near = slice(p_near_ref.shape[1] - rows, p_near_ref.shape[1] - rows + own)
            p = p_near_ref[kv, near, tile] * row_ref[kv, 0:1, tile]
            ds = p * (d_near_ref[kv, near, tile] - row_ref[kv, 1:2, tile])
            own_scr[:own, tile] = ds.astype(jnp.bfloat16)
            ds = jnp.concatenate([ds_ref[kv, start:, tile], own_scr[:own, tile]], axis=0)
            qg = contract(k[start : remote + own], ds, 0, 0) * SCALING
            qg = qg.astype(jnp.bfloat16).T
            att = att_ref[kv, :, tile].T
            for n in range(group):
                h = kv * group + n
                out = (slice(start, start + part), slice(h * HD, (h + 1) * HD))
                att_out[out] = att[n * part : (n + 1) * part]
                qg_out[out] = qg[n * part : (n + 1) * part]
        total_ref[:, key_cols(kv)] = contract(own_scr[...], q_ref[kv], 1, 0) * SCALING
        total_ref[:, value_cols(kv, kv_heads)] = contract(p_ref[kv, remote:], g_ref[kv], 1, 0)


def add_kernel(total_ref, *refs):
    term_refs, (k_ref, v_ref) = refs[:REACH], refs[REACH:]
    width = k_ref.shape[1]
    total = total_ref[...]
    for term_ref in term_refs:
        total = total + term_ref[...].astype(jnp.float32)
    k_ref[...] = total[:, :width].astype(jnp.bfloat16)
    v_ref[...] = total[:, width:].astype(jnp.bfloat16)


def per_device(queries, key_states, value_states, out_grad, doc_lengths):
    rows, width = queries.shape
    kv_width = 2 * key_states.shape[1]
    kv_heads = kv_width // (2 * HD)
    cols = rows * (width // HD // kv_heads)
    keys = (REACH + 1) * rows
    bf16, f32 = jnp.bfloat16, jnp.float32
    array = jax.ShapeDtypeStruct
    narrow = array((rows, kv_width), bf16)
    wide = array((rows, width), bf16)
    tall = array((kv_heads, cols, HD), bf16)
    turned = array((kv_heads, HD, cols), bf16)
    scores = array((kv_heads, keys, cols), bf16)
    dma = pltpu.SemaphoreType.DMA
    work = 2 * HD * rows * cols * kv_heads
    first = (lax.axis_index(("ctx", "rep")) * rows).astype(jnp.int32).reshape(1)
    in_hbm = lambda a: pltpu.with_memory_space_constraint(a, pltpu.MemorySpace.HBM)

    (own,) = call(
        join_kernel,
        "join",
        [narrow],
        [HBM] * 2,
        [in_hbm(key_states), in_hbm(value_states)],
        0,
        [dma((2,))],
    )
    received = {distance: shifted(own, distance) for distance in (4, 3, 1, 2)}
    q, g, qt, gt, low = call(
        load_kernel,
        "load",
        [tall, tall, turned, turned, array((HALVES, cols // HALVES), jnp.int32)],
        [pl.BlockSpec(memory_space=pltpu.SMEM)] + [HBM] * 3,
        [first, in_hbm(doc_lengths.reshape(1, -1)), in_hbm(queries), in_hbm(out_grad)],
        0,
        [
            pltpu.VMEM((1, doc_lengths.shape[0]), jnp.int32),
            pltpu.VMEM(queries.shape, bf16),
            pltpu.VMEM(out_grad.shape, bf16),
            dma((3,)),
        ],
    )
    blocks = [received[distance] if distance else own for distance in ORDER]
    partial = lambda name, before, part, distances: call(
        functools.partial(partial_kernel, distances=distances),
        name,
        [array((kv_heads, len(part) * rows, cols), f32)] * 2
        + [array((kv_heads, 2 + len(before), cols), f32)],
        [VMEM] * (3 + len(before) + len(part)),
        [low, qt, gt] + before + part,
        2 * len(part) * work,
    )
    near = partial("near", [], blocks[FAR + MID :], ORDER[FAR + MID :])
    mid = partial("mid", [near[2]], blocks[FAR : FAR + MID], ORDER[FAR : FAR + MID])
    *terms, att, p, ds, rest = call(
        terms_kernel,
        "terms",
        [narrow] * REACH
        + [turned, scores, array((kv_heads, REACH * rows, cols), bf16)]
        + [array((kv_heads, 2, cols), f32)],
        [VMEM] * (11 + REACH),
        [low, q, g, qt, gt, *mid, *near[:2]] + blocks,
        (2 * FAR + 3 * REACH + 1) * work,
        [pltpu.VMEM((kv_heads, FAR * rows, cols), f32)] * 2,
    )
    returned = [shifted(terms[window(distance)], -distance) for distance in (2, 1, 3, 4)]
    attended, query_grad, total = call(
        own_kernel,
        "own",
        [wide, wide, array((rows, kv_width), f32)],
        [VMEM] * (9 + REACH),
        [q, g, att, p, ds, rest, near[0], near[1]] + blocks,
        (REACH + 3) * work,
        [pltpu.VMEM((rows, cols), bf16)],
    )
    key_grad, value_grad = call(
        add_kernel,
        "add",
        [array(key_states.shape, bf16)] * 2,
        [VMEM] * (1 + REACH),
        [total] + returned,
        0,
    )
    return attended, query_grad, key_grad, value_grad


def solution(mesh):
    split = P(("ctx", "rep"), "tp")
    return jax.shard_map(
        per_device,
        mesh=mesh,
        in_specs=(split, split, split, split, P()),
        out_specs=(split, split, split, split),
        check_vma=False,
    )
```

```python
import functools
import math

import jax
import jax.numpy as jnp
from jax import lax
from jax.experimental import pallas as pl
from jax.experimental.pallas import tpu as pltpu
from jax.sharding import PartitionSpec as P

HD = 128
REACH = 4
ORDER = (4, 3, 1, 2, 0)
FAR, MID = 2, 1
HALVES = 2
MASKED = -1e30
SCALING = 1.0 / math.sqrt(HD)
EXP2_SCALING = SCALING * math.log2(math.e)
VMEM = pl.BlockSpec(memory_space=pltpu.VMEM)
SMEM = pl.BlockSpec(memory_space=pltpu.SMEM)
HBM = pl.BlockSpec(memory_space=pltpu.MemorySpace.HBM)


def shifted(block, distance):
    axes = ("ctx", "rep")
    devices = range(lax.axis_size(axes))
    route = [(i, i + distance) for i in devices if i + distance in devices]
    return lax.ppermute(block, axes, route)


def contract(a, b, dim_a, dim_b):
    return lax.dot_general(
        a, b, (((dim_a,), (dim_b,)), ((), ())), preferred_element_type=jnp.float32
    )


def call(kernel, name, outs, specs, operands, flops, scratch=()):
    size = lambda a: math.prod(a.shape) * jnp.dtype(a.dtype).itemsize
    return pl.pallas_call(
        kernel,
        out_shape=tuple(outs),
        in_specs=specs,
        out_specs=(VMEM,) * len(outs),
        scratch_shapes=list(scratch),
        compiler_params=pltpu.CompilerParams(vmem_limit_bytes=24 << 20),
        cost_estimate=pl.CostEstimate(
            flops=flops,
            bytes_accessed=sum(map(size, (*operands, *outs))),
            transcendentals=0,
        ),
        name=name,
    )(*operands)


def window(distance):
    return ORDER.index(distance)


def key_cols(kv):
    return slice(kv * HD, (kv + 1) * HD)


def value_cols(kv, kv_heads):
    return slice((kv_heads + kv) * HD, (kv_heads + kv + 1) * HD)


def join_kernel(k_hbm, v_hbm, kv_ref, sems):
    width = k_hbm.shape[1]
    copies = [
        pltpu.make_async_copy(k_hbm, kv_ref.at[:, :width], sems.at[0]),
        pltpu.make_async_copy(v_hbm, kv_ref.at[:, width:], sems.at[1]),
    ]
    for copy in copies:
        copy.start()
    for copy in copies:
        copy.wait()


def load_kernel(
    first_ref, lengths_hbm, q_hbm, g_hbm, q_ref, g_ref, qt_ref, gt_ref, low_ref, *scratch
):
    lengths_ref, q_scr, g_scr, sems = scratch
    copies = [
        pltpu.make_async_copy(lengths_hbm, lengths_ref, sems.at[0]),
        pltpu.make_async_copy(q_hbm, q_scr, sems.at[1]),
        pltpu.make_async_copy(g_hbm, g_scr, sems.at[2]),
    ]
    for copy in copies:
        copy.start()
    copies[0].wait()
    rows = q_scr.shape[0]
    kv_heads, cols = q_ref.shape[:2]
    group = cols // rows
    part = rows // HALVES
    lengths = lengths_ref[...]
    docs = lengths.shape[1]
    upto = lax.broadcasted_iota(jnp.int32, (docs, docs), 1) <= lax.broadcasted_iota(
        jnp.int32, (docs, docs), 0
    )
    ends = jnp.sum(jnp.where(upto, lengths, 0), axis=1, keepdims=True)
    first = first_ref[0]
    pos = first + lax.broadcasted_iota(jnp.int32, (docs, rows), 1)
    begins = jnp.max(jnp.where(ends <= pos, ends, 0), axis=0, keepdims=True)
    low = begins - first + REACH * rows
    for half in range(HALVES):
        low_ref[half : half + 1] = jnp.concatenate(
            [low[:, half * part : (half + 1) * part]] * group, axis=1
        )
    for copy, scr, ref, t_ref in (
        (copies[1], q_scr, q_ref, qt_ref),
        (copies[2], g_scr, g_ref, gt_ref),
    ):
        copy.wait()
        for kv in range(kv_heads):
            tall = jnp.concatenate(
                [
                    scr[half * part : (half + 1) * part, h * HD : (h + 1) * HD]
                    for half in range(HALVES)
                    for h in range(kv * group, (kv + 1) * group)
                ],
                axis=0,
            )
            ref[kv] = tall
            t_ref[kv] = tall.T


def own_rows(rows, half):
    return (half + 1) * (rows // HALVES)


def keys_of(distances, rows, cols, skip=0):
    places = [
        lax.broadcasted_iota(jnp.int32, (rows, cols), 0) + (REACH - distance) * rows
        for distance in distances
    ]
    return jnp.concatenate(places, axis=0)[skip:]


def partial_kernel(low_ref, qt_ref, gt_ref, *refs, distances):
    before, kv_refs = refs[: len(refs) - 3 - len(distances)], refs[-3 - len(distances) : -3]
    p_ref, d_ref, stat_ref = refs[-3:]
    rows = kv_refs[0].shape[0]
    kv_heads, _, all_cols = qt_ref.shape
    cols = all_cols // HALVES
    part = rows // HALVES
    for kv in range(kv_heads):
        for half in range(HALVES):
            low = low_ref[half : half + 1]
            own = own_rows(rows, half)
            query = half * part + lax.broadcasted_iota(jnp.int32, (1, cols), 1) % part
            own_key = lax.broadcasted_iota(jnp.int32, (own, cols), 0)
            allowed = jnp.concatenate(
                [
                    keys_of([distance], rows, cols) >= low
                    if distance
                    else (own_key + REACH * rows >= low) & (own_key <= query)
                    for distance in distances
                ],
                axis=0,
            )
            keys = allowed.shape[0]
            tile = slice(half * cols, (half + 1) * cols)
            k = jnp.concatenate([r[:, key_cols(kv)] for r in kv_refs], axis=0)[:keys]
            v = jnp.concatenate([r[:, value_cols(kv, kv_heads)] for r in kv_refs], axis=0)[:keys]
            s = jnp.where(allowed, contract(k, qt_ref[kv, :, tile], 1, 0), MASKED)
            top = jnp.max(s, axis=0, keepdims=True)
            for ref in before:
                top = jnp.maximum(top, ref[kv, 0:1, tile])
            p = jnp.exp2((s - top) * EXP2_SCALING)
            total = jnp.sum(p, axis=0, keepdims=True)
            for ref in before:
                ratio = jnp.exp2((ref[kv, 0:1, tile] - top) * EXP2_SCALING)
                total = total + ratio * ref[kv, 1:2, tile]
                stat_ref[kv, 2:3, tile] = ratio
            p_ref[kv, :keys, tile] = p
            d_ref[kv, :keys, tile] = contract(v, gt_ref[kv, :, tile], 1, 0)
            stat_ref[kv, 0:1, tile] = top
            stat_ref[kv, 1:2, tile] = total


def terms_kernel(low_ref, q_ref, g_ref, qt_ref, gt_ref, *refs):
    blocks = REACH + 1
    (p_mid_ref, d_mid_ref, mid_ref, p_near_ref, d_near_ref), refs = refs[:5], refs[5:]
    kv_refs, refs = refs[:blocks], refs[blocks:]
    term_refs, (att_ref, p_ref, ds_ref, row_ref, p_scr, d_scr) = refs[:REACH], refs[REACH:]
    rows = kv_refs[0].shape[0]
    kv_heads, _, all_cols = qt_ref.shape
    cols = all_cols // HALVES
    part = rows // HALVES
    group_of = [0] * FAR + [1] * MID + [2] * (blocks - FAR - MID)
    firsts = [0, FAR, FAR + MID]
    sources = [(p_scr, d_scr), (p_mid_ref, d_mid_ref), (p_near_ref, d_near_ref)]

    def kept(n, half, base=0):
        start = half * part if n == 0 else 0
        stop = own_rows(rows, half) if n == REACH else rows
        return slice((n - base) * rows + start, (n - base) * rows + stop)

    def held(kv, n, half, which):
        group = group_of[n]
        tile = slice(half * cols, (half + 1) * cols)
        return sources[group][which][kv, kept(n, half, firsts[group]), tile]

    def scores(kv, half, least):
        start = max(half * part, least * rows)
        tile = slice(half * cols, (half + 1) * cols)
        mid_top, mid_sum = mid_ref[kv, 0:1, tile], mid_ref[kv, 1:2, tile]
        inverse = 1.0
        if least < FAR:
            far_refs = kv_refs[least:FAR]
            skip = start - least * rows
            k = jnp.concatenate([r[:, key_cols(kv)] for r in far_refs], axis=0)[skip:]
            v = jnp.concatenate([r[:, value_cols(kv, kv_heads)] for r in far_refs], axis=0)[skip:]
            allowed = keys_of(ORDER[least:FAR], rows, cols, skip) >= low_ref[half : half + 1]
            s = jnp.where(allowed, contract(k, qt_ref[kv, :, tile], 1, 0), MASKED)
            top = jnp.maximum(mid_top, jnp.max(s, axis=0, keepdims=True))
            p = jnp.exp2((s - top) * EXP2_SCALING)
            p_scr[kv, start : FAR * rows, tile] = p
            d_scr[kv, start : FAR * rows, tile] = contract(v, gt_ref[kv, :, tile], 1, 0)
            mid = jnp.exp2((mid_top - top) * EXP2_SCALING)
            inverse = 1.0 / (mid * mid_sum + jnp.sum(p, axis=0, keepdims=True))
            mid = mid * inverse
        else:
            mid = 1.0 / mid_sum
        near = mid * mid_ref[kv, 2:3, tile]
        row_ref[kv, 0:1, tile] = near
        return inverse, mid, near

    def attend(kv, half, scales, least):
        tile = slice(half * cols, (half + 1) * cols)
        parts, v = [], []
        for n in range(least, blocks):
            p_bf = (held(kv, n, half, 0) * scales[group_of[n]]).astype(jnp.bfloat16)
            p_ref[kv, kept(n, half), tile] = p_bf
            parts.append(p_bf)
            v.append(kv_refs[n][kept(n, half, n), value_cols(kv, kv_heads)])
        att = contract(jnp.concatenate(v, axis=0), jnp.concatenate(parts, axis=0), 0, 0)
        att = att.astype(jnp.bfloat16)
        att_ref[kv, :, tile] = att
        gt = gt_ref[kv, :, tile].astype(jnp.float32)
        delta = jnp.sum(gt * att.astype(jnp.float32), axis=0, keepdims=True)
        row_ref[kv, 1:2, tile] = delta
        return delta

    def score_grads(kv, half, scales, delta, least):
        tile = slice(half * cols, (half + 1) * cols)
        for n in range(least, REACH):
            ds = (held(kv, n, half, 0) * scales[group_of[n]]) * (held(kv, n, half, 1) - delta)
            ds_ref[kv, kept(n, half), tile] = ds.astype(jnp.bfloat16)

    def send(kv, least):
        some = slice(least * rows, REACH * rows)
        kg = contract(ds_ref[kv, some], q_ref[kv], 1, 0) * SCALING
        vg = contract(p_ref[kv, some], g_ref[kv], 1, 0)
        for n in range(least, REACH):
            block = slice((n - least) * rows, (n - least + 1) * rows)
            term_refs[n][:, key_cols(kv)] = kg[block].astype(jnp.bfloat16)
            term_refs[n][:, value_cols(kv, kv_heads)] = vg[block].astype(jnp.bfloat16)

    def work(least):
        empty = jnp.zeros((part, cols), jnp.bfloat16)
        for n in range(least):
            term_refs[n][...] = jnp.zeros_like(term_refs[n])
        for kv in range(kv_heads):
            if least:
                ds_ref[kv, : least * rows] = jnp.zeros((least * rows, all_cols), jnp.bfloat16)
            else:
                ds_ref[kv, :part, cols:] = empty
                p_ref[kv, :part, cols:] = empty
            p_ref[kv, (blocks * rows - part) :, :cols] = empty
            scales = [scores(kv, half, least) for half in range(HALVES)]
            deltas = [attend(kv, half, scales[half], least) for half in range(HALVES)]
            for half in range(HALVES):
                score_grads(kv, half, scales[half], deltas[half], least)
            send(kv, least)

    lowest = jnp.min(low_ref[...].astype(jnp.float32))
    reached = [lowest < (n + 1) * rows for n in range(FAR)]
    pl.when(reached[0])(functools.partial(work, 0))
    for n in range(1, FAR):
        pl.when(reached[n] & ~reached[n - 1])(functools.partial(work, n))
    pl.when(~reached[FAR - 1])(functools.partial(work, FAR))


def own_kernel(q_ref, g_ref, att_ref, p_ref, ds_ref, row_ref, p_near_ref, d_near_ref, *refs):
    kv_refs, (att_out, qg_out, total_ref, own_scr) = refs[:-4], refs[-4:]
    rows = kv_refs[0].shape[0]
    kv_heads, all_cols = q_ref.shape[:2]
    group = all_cols // rows
    cols = all_cols // HALVES
    part = rows // HALVES
    remote = REACH * rows
    own_scr[own_rows(rows, 0) :, :cols] = jnp.zeros((rows - part, cols), jnp.bfloat16)
    for kv in range(kv_heads):
        k = jnp.concatenate([r[:, key_cols(kv)] for r in kv_refs], axis=0)
        for half in range(HALVES):
            tile = slice(half * cols, (half + 1) * cols)
            start = half * part
            own = own_rows(rows, half)
            near = slice(p_near_ref.shape[1] - rows, p_near_ref.shape[1] - rows + own)
            p = p_near_ref[kv, near, tile] * row_ref[kv, 0:1, tile]
            ds = p * (d_near_ref[kv, near, tile] - row_ref[kv, 1:2, tile])
            own_scr[:own, tile] = ds.astype(jnp.bfloat16)
            ds = jnp.concatenate([ds_ref[kv, start:, tile], own_scr[:own, tile]], axis=0)
            qg = contract(k[start : remote + own], ds, 0, 0) * SCALING
            qg = qg.astype(jnp.bfloat16).T
            att = att_ref[kv, :, tile].T
            for n in range(group):
                h = kv * group + n
                out = (slice(start, start + part), slice(h * HD, (h + 1) * HD))
                att_out[out] = att[n * part : (n + 1) * part]
                qg_out[out] = qg[n * part : (n + 1) * part]
        total_ref[:, key_cols(kv)] = contract(own_scr[...], q_ref[kv], 1, 0) * SCALING
        total_ref[:, value_cols(kv, kv_heads)] = contract(p_ref[kv, remote:], g_ref[kv], 1, 0)


def add_kernel(total_ref, *refs):
    term_refs, (k_ref, v_ref) = refs[:REACH], refs[REACH:]
    width = k_ref.shape[1]
    total = total_ref[...]
    for term_ref in term_refs:
        total = total + term_ref[...].astype(jnp.float32)
    k_ref[...] = total[:, :width].astype(jnp.bfloat16)
    v_ref[...] = total[:, width:].astype(jnp.bfloat16)


def per_device(queries, key_states, value_states, out_grad, doc_lengths):
    rows, width = queries.shape
    kv_width = 2 * key_states.shape[1]
    kv_heads = kv_width // (2 * HD)
    cols = rows * (width // HD // kv_heads)
    keys = (REACH + 1) * rows
    bf16, f32 = jnp.bfloat16, jnp.float32
    array = jax.ShapeDtypeStruct
    narrow = array((rows, kv_width), bf16)
    wide = array((rows, width), bf16)
    tall = array((kv_heads, cols, HD), bf16)
    turned = array((kv_heads, HD, cols), bf16)
    scores = array((kv_heads, keys, cols), bf16)
    dma = pltpu.SemaphoreType.DMA
    work = 2 * HD * rows * cols * kv_heads
    first = (lax.axis_index(("ctx", "rep")) * rows).astype(jnp.int32).reshape(1)
    in_hbm = lambda a: pltpu.with_memory_space_constraint(a, pltpu.MemorySpace.HBM)

    (own,) = call(
        join_kernel,
        "join",
        [narrow],
        [HBM] * 2,
        [in_hbm(key_states), in_hbm(value_states)],
        0,
        [dma((2,))],
    )
    received = {distance: shifted(own, distance) for distance in (4, 3, 1, 2)}
    q, g, qt, gt, low = call(
        load_kernel,
        "load",
        [tall, tall, turned, turned, array((HALVES, cols // HALVES), jnp.int32)],
        [SMEM] + [HBM] * 3,
        [first, in_hbm(doc_lengths.reshape(1, -1)), in_hbm(queries), in_hbm(out_grad)],
        0,
        [
            pltpu.VMEM((1, doc_lengths.shape[0]), jnp.int32),
            pltpu.VMEM(queries.shape, bf16),
            pltpu.VMEM(out_grad.shape, bf16),
            dma((3,)),
        ],
    )
    blocks = [received[distance] if distance else own for distance in ORDER]
    partial = lambda name, before, part, distances: call(
        functools.partial(partial_kernel, distances=distances),
        name,
        [array((kv_heads, len(part) * rows, cols), f32)] * 2
        + [array((kv_heads, 2 + len(before), cols), f32)],
        [VMEM] * (3 + len(before) + len(part)),
        [low, qt, gt] + before + part,
        2 * len(part) * work,
    )
    near = partial("near", [], blocks[FAR + MID :], ORDER[FAR + MID :])
    mid = partial("mid", [near[2]], blocks[FAR : FAR + MID], ORDER[FAR : FAR + MID])
    *terms, att, p, ds, rest = call(
        terms_kernel,
        "terms",
        [narrow] * REACH
        + [turned, scores, array((kv_heads, REACH * rows, cols), bf16)]
        + [array((kv_heads, 2, cols), f32)],
        [VMEM] * (11 + REACH),
        [low, q, g, qt, gt, *mid, *near[:2]] + blocks,
        (2 * FAR + 3 * REACH + 1) * work,
        [pltpu.VMEM((kv_heads, FAR * rows, cols), f32)] * 2,
    )
    returned = [shifted(terms[window(distance)], -distance) for distance in (2, 1, 3, 4)]
    attended, query_grad, total = call(
        own_kernel,
        "own",
        [wide, wide, array((rows, kv_width), f32)],
        [VMEM] * (9 + REACH),
        [q, g, att, p, ds, rest, near[0], near[1]] + blocks,
        (REACH + 3) * work,
        [pltpu.VMEM((rows, cols), bf16)],
    )
    key_grad, value_grad = call(
        add_kernel,
        "add",
        [array(key_states.shape, bf16)] * 2,
        [VMEM] * (1 + REACH),
        [total] + returned,
        0,
    )
    return attended, query_grad, key_grad, value_grad


def solution(mesh):
    split = P(("ctx", "rep"), "tp")
    return jax.shard_map(
        per_device,
        mesh=mesh,
        in_specs=(split, split, split, split, P()),
        out_specs=(split, split, split, split),
        check_vma=False,
    )
```

```python
import functools
import math

import jax
import jax.numpy as jnp
from jax import lax
from jax.experimental import pallas as pl
from jax.experimental.pallas import tpu as pltpu
from jax.sharding import PartitionSpec as P

HD = 128
REACH = 4
ORDER = (4, 3, 1, 2, 0)
FAR, MID = 2, 1
HALVES = 2
MASKED = -1e30
SCALING = 1.0 / math.sqrt(HD)
EXP2_SCALING = SCALING * math.log2(math.e)
VMEM = pl.BlockSpec(memory_space=pltpu.VMEM)
SMEM = pl.BlockSpec(memory_space=pltpu.SMEM)
HBM = pl.BlockSpec(memory_space=pltpu.MemorySpace.HBM)


def shifted(block, distance):
    axes = ("ctx", "rep")
    devices = range(lax.axis_size(axes))
    route = [(i, i + distance) for i in devices if i + distance in devices]
    return lax.ppermute(block, axes, route)


def contract(a, b, dim_a, dim_b):
    return lax.dot_general(
        a, b, (((dim_a,), (dim_b,)), ((), ())), preferred_element_type=jnp.float32
    )


def call(kernel, name, outs, specs, operands, flops, scratch=()):
    size = lambda a: math.prod(a.shape) * jnp.dtype(a.dtype).itemsize
    return pl.pallas_call(
        kernel,
        out_shape=tuple(outs),
        in_specs=specs,
        out_specs=(VMEM,) * len(outs),
        scratch_shapes=list(scratch),
        compiler_params=pltpu.CompilerParams(vmem_limit_bytes=24 << 20),
        cost_estimate=pl.CostEstimate(
            flops=flops,
            bytes_accessed=sum(map(size, (*operands, *outs))),
            transcendentals=0,
        ),
        name=name,
    )(*operands)


def window(distance):
    return ORDER.index(distance)


def key_cols(kv):
    return slice(kv * HD, (kv + 1) * HD)


def value_cols(kv, kv_heads):
    return slice((kv_heads + kv) * HD, (kv_heads + kv + 1) * HD)


def join_kernel(k_hbm, v_hbm, kv_ref, sems):
    width = k_hbm.shape[1]
    copies = [
        pltpu.make_async_copy(k_hbm, kv_ref.at[:, :width], sems.at[0]),
        pltpu.make_async_copy(v_hbm, kv_ref.at[:, width:], sems.at[1]),
    ]
    for copy in copies:
        copy.start()
    for copy in copies:
        copy.wait()


def load_kernel(
    first_ref, lengths_hbm, q_hbm, g_hbm, q_ref, g_ref, qt_ref, gt_ref, low_ref, *scratch
):
    lengths_ref, q_scr, g_scr, sems = scratch
    copies = [
        pltpu.make_async_copy(lengths_hbm, lengths_ref, sems.at[0]),
        pltpu.make_async_copy(q_hbm, q_scr, sems.at[1]),
        pltpu.make_async_copy(g_hbm, g_scr, sems.at[2]),
    ]
    for copy in copies:
        copy.start()
    copies[0].wait()
    rows = q_scr.shape[0]
    kv_heads, cols = q_ref.shape[:2]
    group = cols // rows
    part = rows // HALVES
    lengths = lengths_ref[...]
    docs = lengths.shape[1]
    upto = lax.broadcasted_iota(jnp.int32, (docs, docs), 1) <= lax.broadcasted_iota(
        jnp.int32, (docs, docs), 0
    )
    ends = jnp.sum(jnp.where(upto, lengths, 0), axis=1, keepdims=True)
    first = first_ref[0]
    pos = first + lax.broadcasted_iota(jnp.int32, (docs, rows), 1)
    begins = jnp.max(jnp.where(ends <= pos, ends, 0), axis=0, keepdims=True)
    low = begins - first + REACH * rows
    for half in range(HALVES):
        low_ref[half : half + 1] = jnp.concatenate(
            [low[:, half * part : (half + 1) * part]] * group, axis=1
        )
    for copy, scr, ref, t_ref in (
        (copies[1], q_scr, q_ref, qt_ref),
        (copies[2], g_scr, g_ref, gt_ref),
    ):
        copy.wait()
        for kv in range(kv_heads):
            tall = jnp.concatenate(
                [
                    scr[half * part : (half + 1) * part, h * HD : (h + 1) * HD]
                    for half in range(HALVES)
                    for h in range(kv * group, (kv + 1) * group)
                ],
                axis=0,
            )
            ref[kv] = tall
            t_ref[kv] = tall.T


def own_rows(rows, half):
    return (half + 1) * (rows // HALVES)


def keys_of(distances, rows, cols, skip=0):
    places = [
        lax.broadcasted_iota(jnp.int32, (rows, cols), 0) + (REACH - distance) * rows
        for distance in distances
    ]
    return jnp.concatenate(places, axis=0)[skip:]


def partial_kernel(low_ref, qt_ref, gt_ref, *refs, distances):
    before, kv_refs = refs[: len(refs) - 3 - len(distances)], refs[-3 - len(distances) : -3]
    p_ref, d_ref, stat_ref = refs[-3:]
    rows = kv_refs[0].shape[0]
    kv_heads, _, all_cols = qt_ref.shape
    cols = all_cols // HALVES
    part = rows // HALVES
    for kv in range(kv_heads):
        for half in range(HALVES):
            low = low_ref[half : half + 1]
            own = own_rows(rows, half)
            query = half * part + lax.broadcasted_iota(jnp.int32, (1, cols), 1) % part
            own_key = lax.broadcasted_iota(jnp.int32, (own, cols), 0)
            allowed = jnp.concatenate(
                [
                    keys_of([distance], rows, cols) >= low
                    if distance
                    else (own_key + REACH * rows >= low) & (own_key <= query)
                    for distance in distances
                ],
                axis=0,
            )
            keys = allowed.shape[0]
            tile = slice(half * cols, (half + 1) * cols)
            k = jnp.concatenate([r[:, key_cols(kv)] for r in kv_refs], axis=0)[:keys]
            v = jnp.concatenate([r[:, value_cols(kv, kv_heads)] for r in kv_refs], axis=0)[:keys]
            s = jnp.where(allowed, contract(k, qt_ref[kv, :, tile], 1, 0), MASKED)
            top = jnp.max(s, axis=0, keepdims=True)
            for ref in before:
                top = jnp.maximum(top, ref[kv, 0:1, tile])
            p = jnp.exp2((s - top) * EXP2_SCALING)
            total = jnp.sum(p, axis=0, keepdims=True)
            for ref in before:
                ratio = jnp.exp2((ref[kv, 0:1, tile] - top) * EXP2_SCALING)
                total = total + ratio * ref[kv, 1:2, tile]
                stat_ref[kv, 2:3, tile] = ratio
            p_ref[kv, :keys, tile] = p
            d_ref[kv, :keys, tile] = contract(v, gt_ref[kv, :, tile], 1, 0)
            stat_ref[kv, 0:1, tile] = top
            stat_ref[kv, 1:2, tile] = total


def terms_kernel(low_ref, q_ref, g_ref, qt_ref, gt_ref, *refs):
    blocks = REACH + 1
    (p_mid_ref, d_mid_ref, mid_ref, p_near_ref, d_near_ref), refs = refs[:5], refs[5:]
    kv_refs, refs = refs[:blocks], refs[blocks:]
    term_refs, (att_ref, p_ref, ds_ref, row_ref, p_scr, d_scr) = refs[:REACH], refs[REACH:]
    rows = kv_refs[0].shape[0]
    kv_heads, _, all_cols = qt_ref.shape
    cols = all_cols // HALVES
    part = rows // HALVES
    group_of = [0] * FAR + [1] * MID + [2] * (blocks - FAR - MID)
    firsts = [0, FAR, FAR + MID]
    sources = [(p_scr, d_scr), (p_mid_ref, d_mid_ref), (p_near_ref, d_near_ref)]

    def kept(n, half, base=0):
        start = half * part if n == 0 else 0
        stop = own_rows(rows, half) if n == REACH else rows
        return slice((n - base) * rows + start, (n - base) * rows + stop)

    def held(kv, n, half, which):
        group = group_of[n]
        tile = slice(half * cols, (half + 1) * cols)
        return sources[group][which][kv, kept(n, half, firsts[group]), tile]

    def scores(kv, half, least):
        start = max(half * part, least * rows)
        tile = slice(half * cols, (half + 1) * cols)
        mid_top, mid_sum = mid_ref[kv, 0:1, tile], mid_ref[kv, 1:2, tile]
        inverse = 1.0
        if least < FAR:
            far_refs = kv_refs[least:FAR]
            skip = start - least * rows
            k = jnp.concatenate([r[:, key_cols(kv)] for r in far_refs], axis=0)[skip:]
            v = jnp.concatenate([r[:, value_cols(kv, kv_heads)] for r in far_refs], axis=0)[skip:]
            allowed = keys_of(ORDER[least:FAR], rows, cols, skip) >= low_ref[half : half + 1]
            s = jnp.where(allowed, contract(k, qt_ref[kv, :, tile], 1, 0), MASKED)
            top = jnp.maximum(mid_top, jnp.max(s, axis=0, keepdims=True))
            p = jnp.exp2((s - top) * EXP2_SCALING)
            p_scr[kv, start : FAR * rows, tile] = p
            d_scr[kv, start : FAR * rows, tile] = contract(v, gt_ref[kv, :, tile], 1, 0)
            mid = jnp.exp2((mid_top - top) * EXP2_SCALING)
            inverse = 1.0 / (mid * mid_sum + jnp.sum(p, axis=0, keepdims=True))
            mid = mid * inverse
        else:
            mid = 1.0 / mid_sum
        near = mid * mid_ref[kv, 2:3, tile]
        row_ref[kv, 0:1, tile] = near
        return inverse, mid, near

    def attend(kv, half, scales, least):
        tile = slice(half * cols, (half + 1) * cols)
        parts, v = [], []
        for n in range(least, blocks):
            p_bf = (held(kv, n, half, 0) * scales[group_of[n]]).astype(jnp.bfloat16)
            p_ref[kv, kept(n, half), tile] = p_bf
            parts.append(p_bf)
            v.append(kv_refs[n][kept(n, half, n), value_cols(kv, kv_heads)])
        att = contract(jnp.concatenate(v, axis=0), jnp.concatenate(parts, axis=0), 0, 0)
        att = att.astype(jnp.bfloat16)
        att_ref[kv, :, tile] = att
        gt = gt_ref[kv, :, tile].astype(jnp.float32)
        delta = jnp.sum(gt * att.astype(jnp.float32), axis=0, keepdims=True)
        row_ref[kv, 1:2, tile] = delta
        return delta

    def score_grads(kv, half, scales, delta, least):
        tile = slice(half * cols, (half + 1) * cols)
        for n in range(least, REACH):
            ds = (held(kv, n, half, 0) * scales[group_of[n]]) * (held(kv, n, half, 1) - delta)
            ds_ref[kv, kept(n, half), tile] = ds.astype(jnp.bfloat16)

    def send(kv, least):
        some = slice(least * rows, REACH * rows)
        kg = contract(ds_ref[kv, some], q_ref[kv], 1, 0) * SCALING
        vg = contract(p_ref[kv, some], g_ref[kv], 1, 0)
        for n in range(least, REACH):
            block = slice((n - least) * rows, (n - least + 1) * rows)
            term_refs[n][:, key_cols(kv)] = kg[block].astype(jnp.bfloat16)
            term_refs[n][:, value_cols(kv, kv_heads)] = vg[block].astype(jnp.bfloat16)

    def work(least):
        empty = jnp.zeros((part, cols), jnp.bfloat16)
        for n in range(least):
            term_refs[n][...] = jnp.zeros_like(term_refs[n])
        for kv in range(kv_heads):
            if least:
                ds_ref[kv, : least * rows] = jnp.zeros((least * rows, all_cols), jnp.bfloat16)
            else:
                ds_ref[kv, :part, cols:] = empty
                p_ref[kv, :part, cols:] = empty
            p_ref[kv, (blocks * rows - part) :, :cols] = empty
            scales = [scores(kv, half, least) for half in range(HALVES)]
            deltas = [attend(kv, half, scales[half], least) for half in range(HALVES)]
            for half in range(HALVES):
                score_grads(kv, half, scales[half], deltas[half], least)
            send(kv, least)

    lowest = jnp.min(low_ref[...].astype(jnp.float32))
    reached = [lowest < (n + 1) * rows for n in range(FAR)]
    pl.when(reached[0])(functools.partial(work, 0))
    for n in range(1, FAR):
        pl.when(reached[n] & ~reached[n - 1])(functools.partial(work, n))
    pl.when(~reached[FAR - 1])(functools.partial(work, FAR))


def own_kernel(q_ref, g_ref, att_ref, p_ref, ds_ref, row_ref, p_near_ref, d_near_ref, *refs):
    kv_refs, (att_out, qg_out, total_ref, own_scr) = refs[:-4], refs[-4:]
    rows = kv_refs[0].shape[0]
    kv_heads, all_cols = q_ref.shape[:2]
    group = all_cols // rows
    cols = all_cols // HALVES
    part = rows // HALVES
    remote = REACH * rows
    own_scr[own_rows(rows, 0) :, :cols] = jnp.zeros((rows - part, cols), jnp.bfloat16)
    for kv in range(kv_heads):
        k = jnp.concatenate([r[:, key_cols(kv)] for r in kv_refs], axis=0)
        for half in range(HALVES):
            tile = slice(half * cols, (half + 1) * cols)
            start = half * part
            own = own_rows(rows, half)
            near = slice(p_near_ref.shape[1] - rows, p_near_ref.shape[1] - rows + own)
            p = p_near_ref[kv, near, tile] * row_ref[kv, 0:1, tile]
            ds = p * (d_near_ref[kv, near, tile] - row_ref[kv, 1:2, tile])
            own_scr[:own, tile] = ds.astype(jnp.bfloat16)
            ds = jnp.concatenate([ds_ref[kv, start:, tile], own_scr[:own, tile]], axis=0)
            qg = contract(k[start : remote + own], ds, 0, 0) * SCALING
            qg = qg.astype(jnp.bfloat16).T
            att = att_ref[kv, :, tile].T
            for n in range(group):
                h = kv * group + n
                out = (slice(start, start + part), slice(h * HD, (h + 1) * HD))
                att_out[out] = att[n * part : (n + 1) * part]
                qg_out[out] = qg[n * part : (n + 1) * part]
        total_ref[:, key_cols(kv)] = contract(own_scr[...], q_ref[kv], 1, 0) * SCALING
        total_ref[:, value_cols(kv, kv_heads)] = contract(p_ref[kv, remote:], g_ref[kv], 1, 0)


def add_kernel(total_ref, *refs):
    term_refs, (k_ref, v_ref) = refs[:REACH], refs[REACH:]
    width = k_ref.shape[1]
    total = total_ref[...]
    for term_ref in term_refs:
        total = total + term_ref[...].astype(jnp.float32)
    k_ref[...] = total[:, :width].astype(jnp.bfloat16)
    v_ref[...] = total[:, width:].astype(jnp.bfloat16)


def per_device(queries, key_states, value_states, out_grad, doc_lengths):
    rows, width = queries.shape
    kv_width = 2 * key_states.shape[1]
    kv_heads = kv_width // (2 * HD)
    cols = rows * (width // HD // kv_heads)
    keys = (REACH + 1) * rows
    bf16, f32 = jnp.bfloat16, jnp.float32
    array = jax.ShapeDtypeStruct
    narrow = array((rows, kv_width), bf16)
    wide = array((rows, width), bf16)
    tall = array((kv_heads, cols, HD), bf16)
    turned = array((kv_heads, HD, cols), bf16)
    scores = array((kv_heads, keys, cols), bf16)
    dma = pltpu.SemaphoreType.DMA
    work = 2 * HD * rows * cols * kv_heads
    first = (lax.axis_index(("ctx", "rep")) * rows).astype(jnp.int32).reshape(1)
    in_hbm = lambda a: pltpu.with_memory_space_constraint(a, pltpu.MemorySpace.HBM)

    (own,) = call(
        join_kernel,
        "join",
        [narrow],
        [HBM] * 2,
        [in_hbm(key_states), in_hbm(value_states)],
        0,
        [dma((2,))],
    )
    received = {distance: shifted(own, distance) for distance in (4, 3, 1, 2)}
    q, g, qt, gt, low = call(
        load_kernel,
        "load",
        [tall, tall, turned, turned, array((HALVES, cols // HALVES), jnp.int32)],
        [SMEM] + [HBM] * 3,
        [first, in_hbm(doc_lengths.reshape(1, -1)), in_hbm(queries), in_hbm(out_grad)],
        0,
        [
            pltpu.VMEM((1, doc_lengths.shape[0]), jnp.int32),
            pltpu.VMEM(queries.shape, bf16),
            pltpu.VMEM(out_grad.shape, bf16),
            dma((3,)),
        ],
    )
    blocks = [received[distance] if distance else own for distance in ORDER]
    partial = lambda name, before, part, distances: call(
        functools.partial(partial_kernel, distances=distances),
        name,
        [array((kv_heads, len(part) * rows, cols), f32)] * 2
        + [array((kv_heads, 2 + len(before), cols), f32)],
        [VMEM] * (3 + len(before) + len(part)),
        [low, qt, gt] + before + part,
        2 * len(part) * work,
    )
    near = partial("near", [], blocks[FAR + MID :], ORDER[FAR + MID :])
    mid = partial("mid", [near[2]], blocks[FAR : FAR + MID], ORDER[FAR : FAR + MID])
    *terms, att, p, ds, rest = call(
        terms_kernel,
        "terms",
        [narrow] * REACH
        + [turned, scores, array((kv_heads, REACH * rows, cols), bf16)]
        + [array((kv_heads, 2, cols), f32)],
        [VMEM] * (11 + REACH),
        [low, q, g, qt, gt, *mid, *near[:2]] + blocks,
        (2 * FAR + 3 * REACH + 1) * work,
        [pltpu.VMEM((kv_heads, FAR * rows, cols), f32)] * 2,
    )
    returned = [shifted(terms[window(distance)], -distance) for distance in (2, 1, 4, 3)]
    attended, query_grad, total = call(
        own_kernel,
        "own",
        [wide, wide, array((rows, kv_width), f32)],
        [VMEM] * (9 + REACH),
        [q, g, att, p, ds, rest, near[0], near[1]] + blocks,
        (REACH + 3) * work,
        [pltpu.VMEM((rows, cols), bf16)],
    )
    key_grad, value_grad = call(
        add_kernel,
        "add",
        [array(key_states.shape, bf16)] * 2,
        [VMEM] * (1 + REACH),
        [total] + returned,
        0,
    )
    return attended, query_grad, key_grad, value_grad


def solution(mesh):
    split = P(("ctx", "rep"), "tp")
    return jax.shard_map(
        per_device,
        mesh=mesh,
        in_specs=(split, split, split, split, P()),
        out_specs=(split, split, split, split),
        check_vma=False,
    )
```

```python
import functools
import math

import jax
import jax.numpy as jnp
from jax import lax
from jax.experimental import pallas as pl
from jax.experimental.pallas import tpu as pltpu
from jax.sharding import PartitionSpec as P

HD = 128
REACH = 4
ORDER = (4, 3, 1, 2, 0)
FAR, MID = 2, 1
HALVES = 2
MASKED = -1e30
SCALING = 1.0 / math.sqrt(HD)
EXP2_SCALING = SCALING * math.log2(math.e)
VMEM = pl.BlockSpec(memory_space=pltpu.VMEM)
SMEM = pl.BlockSpec(memory_space=pltpu.SMEM)
HBM = pl.BlockSpec(memory_space=pltpu.MemorySpace.HBM)


def shifted(block, distance):
    axes = ("ctx", "rep")
    devices = range(lax.axis_size(axes))
    route = [(i, i + distance) for i in devices if i + distance in devices]
    return lax.ppermute(block, axes, route)


def contract(a, b, dim_a, dim_b):
    return lax.dot_general(
        a, b, (((dim_a,), (dim_b,)), ((), ())), preferred_element_type=jnp.float32
    )


def call(kernel, name, outs, specs, operands, flops, scratch=()):
    size = lambda a: math.prod(a.shape) * jnp.dtype(a.dtype).itemsize
    return pl.pallas_call(
        kernel,
        out_shape=tuple(outs),
        in_specs=specs,
        out_specs=(VMEM,) * len(outs),
        scratch_shapes=list(scratch),
        compiler_params=pltpu.CompilerParams(vmem_limit_bytes=24 << 20),
        cost_estimate=pl.CostEstimate(
            flops=flops,
            bytes_accessed=sum(map(size, (*operands, *outs))),
            transcendentals=0,
        ),
        name=name,
    )(*operands)


def window(distance):
    return ORDER.index(distance)


def key_cols(kv):
    return slice(kv * HD, (kv + 1) * HD)


def value_cols(kv, kv_heads):
    return slice((kv_heads + kv) * HD, (kv_heads + kv + 1) * HD)


def join_kernel(k_hbm, v_hbm, kv_ref, sems):
    width = k_hbm.shape[1]
    copies = [
        pltpu.make_async_copy(k_hbm, kv_ref.at[:, :width], sems.at[0]),
        pltpu.make_async_copy(v_hbm, kv_ref.at[:, width:], sems.at[1]),
    ]
    for copy in copies:
        copy.start()
    for copy in copies:
        copy.wait()


def load_kernel(
    first_ref, lengths_hbm, q_hbm, g_hbm, q_ref, g_ref, qt_ref, gt_ref, low_ref, *scratch
):
    lengths_ref, q_scr, g_scr, sems = scratch
    copies = [
        pltpu.make_async_copy(lengths_hbm, lengths_ref, sems.at[0]),
        pltpu.make_async_copy(q_hbm, q_scr, sems.at[1]),
        pltpu.make_async_copy(g_hbm, g_scr, sems.at[2]),
    ]
    for copy in copies:
        copy.start()
    copies[0].wait()
    rows = q_scr.shape[0]
    kv_heads, cols = q_ref.shape[:2]
    group = cols // rows
    part = rows // HALVES
    lengths = lengths_ref[...]
    docs = lengths.shape[1]
    upto = lax.broadcasted_iota(jnp.int32, (docs, docs), 1) <= lax.broadcasted_iota(
        jnp.int32, (docs, docs), 0
    )
    ends = jnp.sum(jnp.where(upto, lengths, 0), axis=1, keepdims=True)
    first = first_ref[0]
    pos = first + lax.broadcasted_iota(jnp.int32, (docs, rows), 1)
    begins = jnp.max(jnp.where(ends <= pos, ends, 0), axis=0, keepdims=True)
    low = begins - first + REACH * rows
    for half in range(HALVES):
        low_ref[half : half + 1] = jnp.concatenate(
            [low[:, half * part : (half + 1) * part]] * group, axis=1
        )
    for copy, scr, ref, t_ref in (
        (copies[1], q_scr, q_ref, qt_ref),
        (copies[2], g_scr, g_ref, gt_ref),
    ):
        copy.wait()
        for kv in range(kv_heads):
            tall = jnp.concatenate(
                [
                    scr[half * part : (half + 1) * part, h * HD : (h + 1) * HD]
                    for half in range(HALVES)
                    for h in range(kv * group, (kv + 1) * group)
                ],
                axis=0,
            )
            ref[kv] = tall
            t_ref[kv] = tall.T


def own_rows(rows, half):
    return (half + 1) * (rows // HALVES)


def keys_of(distances, rows, cols, skip=0):
    places = [
        lax.broadcasted_iota(jnp.int32, (rows, cols), 0) + (REACH - distance) * rows
        for distance in distances
    ]
    return jnp.concatenate(places, axis=0)[skip:]


def partial_kernel(low_ref, qt_ref, gt_ref, *refs, distances):
    before, kv_refs = refs[: len(refs) - 3 - len(distances)], refs[-3 - len(distances) : -3]
    p_ref, d_ref, stat_ref = refs[-3:]
    rows = kv_refs[0].shape[0]
    kv_heads, _, all_cols = qt_ref.shape
    cols = all_cols // HALVES
    part = rows // HALVES
    for kv in range(kv_heads):
        for half in range(HALVES):
            low = low_ref[half : half + 1]
            own = own_rows(rows, half)
            query = half * part + lax.broadcasted_iota(jnp.int32, (1, cols), 1) % part
            own_key = lax.broadcasted_iota(jnp.int32, (own, cols), 0)
            allowed = jnp.concatenate(
                [
                    keys_of([distance], rows, cols) >= low
                    if distance
                    else (own_key + REACH * rows >= low) & (own_key <= query)
                    for distance in distances
                ],
                axis=0,
            )
            keys = allowed.shape[0]
            tile = slice(half * cols, (half + 1) * cols)
            k = jnp.concatenate([r[:, key_cols(kv)] for r in kv_refs], axis=0)[:keys]
            v = jnp.concatenate([r[:, value_cols(kv, kv_heads)] for r in kv_refs], axis=0)[:keys]
            s = jnp.where(allowed, contract(k, qt_ref[kv, :, tile], 1, 0), MASKED)
            top = jnp.max(s, axis=0, keepdims=True)
            for ref in before:
                top = jnp.maximum(top, ref[kv, 0:1, tile])
            p = jnp.exp2((s - top) * EXP2_SCALING)
            total = jnp.sum(p, axis=0, keepdims=True)
            for ref in before:
                ratio = jnp.exp2((ref[kv, 0:1, tile] - top) * EXP2_SCALING)
                total = total + ratio * ref[kv, 1:2, tile]
                stat_ref[kv, 2:3, tile] = ratio
            p_ref[kv, :keys, tile] = p
            d_ref[kv, :keys, tile] = contract(v, gt_ref[kv, :, tile], 1, 0)
            stat_ref[kv, 0:1, tile] = top
            stat_ref[kv, 1:2, tile] = total


def terms_kernel(low_ref, q_ref, g_ref, qt_ref, gt_ref, *refs):
    blocks = REACH + 1
    (p_mid_ref, d_mid_ref, mid_ref, p_near_ref, d_near_ref), refs = refs[:5], refs[5:]
    kv_refs, refs = refs[:blocks], refs[blocks:]
    term_refs, (att_ref, p_ref, ds_ref, row_ref, p_scr, d_scr) = refs[:REACH], refs[REACH:]
    rows = kv_refs[0].shape[0]
    kv_heads, _, all_cols = qt_ref.shape
    cols = all_cols // HALVES
    part = rows // HALVES
    group_of = [0] * FAR + [1] * MID + [2] * (blocks - FAR - MID)
    firsts = [0, FAR, FAR + MID]
    sources = [(p_scr, d_scr), (p_mid_ref, d_mid_ref), (p_near_ref, d_near_ref)]

    def kept(n, half, base=0):
        start = half * part if n == 0 else 0
        stop = own_rows(rows, half) if n == REACH else rows
        return slice((n - base) * rows + start, (n - base) * rows + stop)

    def held(kv, n, half, which):
        group = group_of[n]
        tile = slice(half * cols, (half + 1) * cols)
        return sources[group][which][kv, kept(n, half, firsts[group]), tile]

    def scores(kv, half, least):
        start = max(half * part, least * rows)
        tile = slice(half * cols, (half + 1) * cols)
        mid_top, mid_sum = mid_ref[kv, 0:1, tile], mid_ref[kv, 1:2, tile]
        inverse = 1.0
        if least < FAR:
            far_refs = kv_refs[least:FAR]
            skip = start - least * rows
            k = jnp.concatenate([r[:, key_cols(kv)] for r in far_refs], axis=0)[skip:]
            v = jnp.concatenate([r[:, value_cols(kv, kv_heads)] for r in far_refs], axis=0)[skip:]
            allowed = keys_of(ORDER[least:FAR], rows, cols, skip) >= low_ref[half : half + 1]
            s = jnp.where(allowed, contract(k, qt_ref[kv, :, tile], 1, 0), MASKED)
            top = jnp.maximum(mid_top, jnp.max(s, axis=0, keepdims=True))
            p = jnp.exp2((s - top) * EXP2_SCALING)
            p_scr[kv, start : FAR * rows, tile] = p
            d_scr[kv, start : FAR * rows, tile] = contract(v, gt_ref[kv, :, tile], 1, 0)
            mid = jnp.exp2((mid_top - top) * EXP2_SCALING)
            inverse = 1.0 / (mid * mid_sum + jnp.sum(p, axis=0, keepdims=True))
            mid = mid * inverse
        else:
            mid = 1.0 / mid_sum
        near = mid * mid_ref[kv, 2:3, tile]
        row_ref[kv, 0:1, tile] = near
        return inverse, mid, near

    def attend(kv, half, scales, least):
        tile = slice(half * cols, (half + 1) * cols)
        parts, v = [], []
        for n in range(least, blocks):
            p_bf = (held(kv, n, half, 0) * scales[group_of[n]]).astype(jnp.bfloat16)
            p_ref[kv, kept(n, half), tile] = p_bf
            parts.append(p_bf)
            v.append(kv_refs[n][kept(n, half, n), value_cols(kv, kv_heads)])
        att = contract(jnp.concatenate(v, axis=0), jnp.concatenate(parts, axis=0), 0, 0)
        att = att.astype(jnp.bfloat16)
        att_ref[kv, :, tile] = att
        gt = gt_ref[kv, :, tile].astype(jnp.float32)
        delta = jnp.sum(gt * att.astype(jnp.float32), axis=0, keepdims=True)
        row_ref[kv, 1:2, tile] = delta
        return delta

    def score_grads(kv, half, scales, delta, least):
        tile = slice(half * cols, (half + 1) * cols)
        for n in range(least, REACH):
            ds = (held(kv, n, half, 0) * scales[group_of[n]]) * (held(kv, n, half, 1) - delta)
            ds_ref[kv, kept(n, half), tile] = ds.astype(jnp.bfloat16)

    def send(kv, least):
        some = slice(least * rows, REACH * rows)
        kg = contract(ds_ref[kv, some], q_ref[kv], 1, 0) * SCALING
        vg = contract(p_ref[kv, some], g_ref[kv], 1, 0)
        for n in range(least, REACH):
            block = slice((n - least) * rows, (n - least + 1) * rows)
            term_refs[n][:, key_cols(kv)] = kg[block].astype(jnp.bfloat16)
            term_refs[n][:, value_cols(kv, kv_heads)] = vg[block].astype(jnp.bfloat16)

    def work(least):
        empty = jnp.zeros((part, cols), jnp.bfloat16)
        for n in range(least):
            term_refs[n][...] = jnp.zeros_like(term_refs[n])
        for kv in range(kv_heads):
            if least:
                ds_ref[kv, : least * rows] = jnp.zeros((least * rows, all_cols), jnp.bfloat16)
            else:
                ds_ref[kv, :part, cols:] = empty
                p_ref[kv, :part, cols:] = empty
            p_ref[kv, (blocks * rows - part) :, :cols] = empty
            scales = [scores(kv, half, least) for half in range(HALVES)]
            deltas = [attend(kv, half, scales[half], least) for half in range(HALVES)]
            for half in range(HALVES):
                score_grads(kv, half, scales[half], deltas[half], least)
            send(kv, least)

    lowest = jnp.min(low_ref[...].astype(jnp.float32))
    reached = [lowest < (n + 1) * rows for n in range(FAR)]
    pl.when(reached[0])(functools.partial(work, 0))
    for n in range(1, FAR):
        pl.when(reached[n] & ~reached[n - 1])(functools.partial(work, n))
    pl.when(~reached[FAR - 1])(functools.partial(work, FAR))


def own_kernel(q_ref, g_ref, att_ref, p_ref, ds_ref, row_ref, p_near_ref, d_near_ref, *refs):
    kv_refs, (att_out, qg_out, total_ref, own_scr) = refs[:-4], refs[-4:]
    rows = kv_refs[0].shape[0]
    kv_heads, all_cols = q_ref.shape[:2]
    group = all_cols // rows
    cols = all_cols // HALVES
    part = rows // HALVES
    remote = REACH * rows
    own_scr[own_rows(rows, 0) :, :cols] = jnp.zeros((rows - part, cols), jnp.bfloat16)
    for kv in range(kv_heads):
        k = jnp.concatenate([r[:, key_cols(kv)] for r in kv_refs], axis=0)
        for half in range(HALVES):
            tile = slice(half * cols, (half + 1) * cols)
            start = half * part
            own = own_rows(rows, half)
            near = slice(p_near_ref.shape[1] - rows, p_near_ref.shape[1] - rows + own)
            p = p_near_ref[kv, near, tile] * row_ref[kv, 0:1, tile]
            ds = p * (d_near_ref[kv, near, tile] - row_ref[kv, 1:2, tile])
            own_scr[:own, tile] = ds.astype(jnp.bfloat16)
            ds = jnp.concatenate([ds_ref[kv, start:, tile], own_scr[:own, tile]], axis=0)
            qg = contract(k[start : remote + own], ds, 0, 0) * SCALING
            qg = qg.astype(jnp.bfloat16).T
            att = att_ref[kv, :, tile].T
            for n in range(group):
                h = kv * group + n
                out = (slice(start, start + part), slice(h * HD, (h + 1) * HD))
                att_out[out] = att[n * part : (n + 1) * part]
                qg_out[out] = qg[n * part : (n + 1) * part]
        total_ref[:, key_cols(kv)] = contract(own_scr[...], q_ref[kv], 1, 0) * SCALING
        total_ref[:, value_cols(kv, kv_heads)] = contract(p_ref[kv, remote:], g_ref[kv], 1, 0)


def sum_kernel(total_ref, *refs):
    total = total_ref[...]
    for term_ref in refs[:-1]:
        total = total + term_ref[...].astype(jnp.float32)
    refs[-1][...] = total


def add_kernel(total_ref, term_ref, k_ref, v_ref):
    width = k_ref.shape[1]
    total = total_ref[...] + term_ref[...].astype(jnp.float32)
    k_ref[...] = total[:, :width].astype(jnp.bfloat16)
    v_ref[...] = total[:, width:].astype(jnp.bfloat16)


def per_device(queries, key_states, value_states, out_grad, doc_lengths):
    rows, width = queries.shape
    kv_width = 2 * key_states.shape[1]
    kv_heads = kv_width // (2 * HD)
    cols = rows * (width // HD // kv_heads)
    keys = (REACH + 1) * rows
    bf16, f32 = jnp.bfloat16, jnp.float32
    array = jax.ShapeDtypeStruct
    narrow = array((rows, kv_width), bf16)
    wide = array((rows, width), bf16)
    tall = array((kv_heads, cols, HD), bf16)
    turned = array((kv_heads, HD, cols), bf16)
    scores = array((kv_heads, keys, cols), bf16)
    dma = pltpu.SemaphoreType.DMA
    work = 2 * HD * rows * cols * kv_heads
    first = (lax.axis_index(("ctx", "rep")) * rows).astype(jnp.int32).reshape(1)
    in_hbm = lambda a: pltpu.with_memory_space_constraint(a, pltpu.MemorySpace.HBM)

    (own,) = call(
        join_kernel,
        "join",
        [narrow],
        [HBM] * 2,
        [in_hbm(key_states), in_hbm(value_states)],
        0,
        [dma((2,))],
    )
    received = {distance: shifted(own, distance) for distance in (4, 3, 1, 2)}
    q, g, qt, gt, low = call(
        load_kernel,
        "load",
        [tall, tall, turned, turned, array((HALVES, cols // HALVES), jnp.int32)],
        [SMEM] + [HBM] * 3,
        [first, in_hbm(doc_lengths.reshape(1, -1)), in_hbm(queries), in_hbm(out_grad)],
        0,
        [
            pltpu.VMEM((1, doc_lengths.shape[0]), jnp.int32),
            pltpu.VMEM(queries.shape, bf16),
            pltpu.VMEM(out_grad.shape, bf16),
            dma((3,)),
        ],
    )
    blocks = [received[distance] if distance else own for distance in ORDER]
    partial = lambda name, before, part, distances: call(
        functools.partial(partial_kernel, distances=distances),
        name,
        [array((kv_heads, len(part) * rows, cols), f32)] * 2
        + [array((kv_heads, 2 + len(before), cols), f32)],
        [VMEM] * (3 + len(before) + len(part)),
        [low, qt, gt] + before + part,
        2 * len(part) * work,
    )
    near = partial("near", [], blocks[FAR + MID :], ORDER[FAR + MID :])
    mid = partial("mid", [near[2]], blocks[FAR : FAR + MID], ORDER[FAR : FAR + MID])
    *terms, att, p, ds, rest = call(
        terms_kernel,
        "terms",
        [narrow] * REACH
        + [turned, scores, array((kv_heads, REACH * rows, cols), bf16)]
        + [array((kv_heads, 2, cols), f32)],
        [VMEM] * (11 + REACH),
        [low, q, g, qt, gt, *mid, *near[:2]] + blocks,
        (2 * FAR + 3 * REACH + 1) * work,
        [pltpu.VMEM((kv_heads, FAR * rows, cols), f32)] * 2,
    )
    returned = [shifted(terms[window(distance)], -distance) for distance in (2, 1, 3, 4)]
    attended, query_grad, total = call(
        own_kernel,
        "own",
        [wide, wide, array((rows, kv_width), f32)],
        [VMEM] * (9 + REACH),
        [q, g, att, p, ds, rest, near[0], near[1]] + blocks,
        (REACH + 3) * work,
        [pltpu.VMEM((rows, cols), bf16)],
    )
    (total,) = call(
        sum_kernel,
        "sum",
        [array((rows, kv_width), f32)],
        [VMEM] * REACH,
        [total] + returned[:-1],
        0,
    )
    key_grad, value_grad = call(
        add_kernel,
        "add",
        [array(key_states.shape, bf16)] * 2,
        [VMEM] * 2,
        [total, returned[-1]],
        0,
    )
    return attended, query_grad, key_grad, value_grad


def solution(mesh):
    split = P(("ctx", "rep"), "tp")
    return jax.shard_map(
        per_device,
        mesh=mesh,
        in_specs=(split, split, split, split, P()),
        out_specs=(split, split, split, split),
        check_vma=False,
    )
```
